256 devices in a mesh: sector: 32 (over y_hi, z, core), col: 8 (over x, y_lo).
Axes of the slice: x: 4, y: 4 (y_hi: 2, y_lo: 2; y = y_hi * 2 + y_lo), z: 8, core: 2. Of those that a mesh axis runs over, the one named last changes fastest.
Arguments:
- prev_nodes: float32 [4, 2, 512, 128, 256], P(None, None, 'col', 'sector'), may hold values from -6 to 6
- stiffness: float32 [128, 256], P('sector'), may hold values from 1 to 4
- aero_coef: bfloat16 [32, 128, 128], replicated, may hold values from -0.125 to 0.125
- offset_slot: int32 [128], replicated, may hold values from 0 to 31
- contact_left: int32 [128, 128], P('sector'), may hold values from 0 to 255
- contact_right: int32 [128, 128], P('sector'), may hold values from 0 to 255
- contact_mask: int32 [128, 128], P('sector'), may hold values from 0 to 2
Outputs:
- scaled_end: float32 [2, 512, 128, 256], P(None, 'col', 'sector')
- growth: float32 [], replicated
The draws below stay inside these ranges and needn't reach their ends.
All inputs are finite; a program needn't handle non-finite values.
Results may differ from the reference program's by a relative error of at most 0.0012.
Values may be sent and summed in bfloat16 or wider, within the bound.
A program may use at most 128 MiB of HBM per device.

```python
import math
import jax
import jax.numpy as jnp
from jax import lax

SECTORS = 128
COLS = 512
DOF = 256
AERO = 128
NC = 128
KC = 32
NODES = 4


def set_ends(drawn, own_key, least, largest):
    spot = [jax.random.randint(jax.random.fold_in(own_key, axis), (), 0, length) for axis, length in enumerate(drawn.shape)]
    main_axis = drawn.shape.index(max(drawn.shape))
    neighbour = spot[:main_axis] + [(spot[main_axis] + 1) % drawn.shape[main_axis]] + spot[main_axis + 1:]
    return drawn.at[tuple(spot)].set(least).at[tuple(neighbour)].set(largest)


def levels(own_key, dims, shards, low, high):
    def one(dim, blocks):
        steps = jax.random.uniform(jax.random.fold_in(jax.random.fold_in(own_key, 6), dim), (blocks,), jnp.float32, low / len(shards), high / len(shards))
        return jnp.repeat(jnp.exp(steps), dims[dim] // blocks).reshape((-1,) + (1,) * (len(dims) - dim - 1))

    loudness = one(*shards[0])
    for cut in shards[1:]:
        loudness = loudness * one(*cut)
    return loudness


def scatter_about(rng, extent, scale, reach, split=(), kind=jnp.bfloat16):
    factor_of = levels(rng, extent, split, -0.22, 0.18) if split else 1.0
    entries = jax.random.normal(rng, extent, jnp.float32) * scale * factor_of
    return jnp.minimum(jnp.maximum(entries, -reach), reach).astype(kind)


def setup_inputs(seed: int = 0) -> dict:
    key_of = jax.random.split(jax.random.key(seed), 8)
    return {
        "prev_nodes": scatter_about(key_of[0], (NODES, 2, COLS, SECTORS, DOF), 1.0, 6.0, ((2, 8), (3, 32)), jnp.float32),
        "stiffness": jnp.clip(jnp.exp(math.log(4.0) - 1.3862944 * jax.random.uniform(key_of[1], (SECTORS, DOF), jnp.float32) ** levels(key_of[1], (SECTORS, DOF), ((0, 32),), -0.2, 0.2)), 1.0, 4.0),
        "aero_coef": scatter_about(key_of[2], (KC, AERO, AERO), (AERO * 16) ** -0.5, 0.125),
        "offset_slot": set_ends(jax.random.randint(key_of[3], (SECTORS,), 0, KC), jax.random.fold_in(key_of[3], 1), 0, KC - 1).astype(jnp.int32),
        "contact_left": set_ends(jax.random.randint(key_of[4], (SECTORS, NC), 0, DOF), jax.random.fold_in(key_of[4], 1), 0, DOF - 1).astype(jnp.int32),
        "contact_right": set_ends(jax.random.randint(key_of[5], (SECTORS, NC), 0, DOF), jax.random.fold_in(key_of[5], 1), 0, DOF - 1).astype(jnp.int32),
        "contact_mask": set_ends(jax.random.randint(key_of[6], (SECTORS, NC), 0, 3), jax.random.fold_in(key_of[6], 1), 0, 2).astype(jnp.int32),
    }


time_step = 0.25
coupling = 0.5
damping = 0.1
k_stick = 4.0
k_slip = 1.0

def quad_tables():
    root = 1.0 / math.sqrt(5.0)
    tau = [0.0, (1.0 - root) / 2.0, (1.0 + root) / 2.0, 1.0]
    table = []
    for m in range(3):
        table_row = []
        for j in range(4):
            coeffs = [1.0]
            scale = 1.0
            for k in range(4):
                if k != j:
                    widened = [0.0] * (len(coeffs) + 1)
                    for power in range(len(coeffs)):
                        widened[power + 1] = widened[power + 1] + coeffs[power]
                        widened[power] = widened[power] - tau[k] * coeffs[power]
                    coeffs = widened
                    scale = scale * (tau[j] - tau[k])
            integral = 0.0
            for power in range(len(coeffs)):
                integral = integral + coeffs[power] * (tau[m + 1] ** (power + 1) - tau[m] ** (power + 1)) / (power + 1)
            table_row.append(integral / scale * time_step)
        table.append(table_row)
    steps = [(tau[m + 1] - tau[m]) * time_step for m in range(3)]
    return (table, steps)

def add_rows(force, rows, values):
    return jax.vmap(lambda f, r, x: f.at[:, r].add(x), in_axes=(1, 0, 1), out_axes=1)(force, rows, values)

def influence(surface, coef_rows):
    count = surface.shape[1]
    surf32 = surface.astype(jnp.float32)
    coef32 = coef_rows.astype(jnp.float32)
    source = jnp.arange(count, dtype=jnp.int32)

    def one_target(target):
        picked = coef32[(source - target) % count]
        return jnp.einsum('ctb,tba->ca', surf32, picked)
    loads = lax.map(one_target, source)
    return jnp.transpose(loads, (1, 0, 2))

def evaluate(state, stiffness, coef_rows, contact_left, contact_right, kmask):
    displace, velocity = (state[0], state[1])
    padded = jnp.pad(displace, ((0, 0), (0, 0), (1, 1)))
    elastic = stiffness[None] * displace - coupling * (padded[..., :-2] + padded[..., 2:])
    aero_width = coef_rows.shape[1]
    surface = displace[..., :aero_width].astype(jnp.bfloat16)
    loads = influence(surface, coef_rows)
    left_vals = jnp.take_along_axis(displace, contact_left[None], axis=2)
    right_vals = jnp.take_along_axis(displace, contact_right[None], axis=2)
    partner = jnp.roll(right_vals, -1, axis=1)
    react = kmask[None] * (left_vals - partner)
    force = jnp.zeros_like(displace)
    force = add_rows(force, contact_left, -react)
    force = add_rows(force, contact_right, jnp.roll(react, 1, axis=1))
    loads_full = jnp.pad(loads, ((0, 0), (0, 0), (0, displace.shape[2] - aero_width)))
    accel = -elastic - damping * velocity + force + loads_full
    return jnp.stack([velocity, accel])

def reference(prev_nodes, stiffness, aero_coef, offset_slot, contact_left, contact_right, contact_mask):
    table, steps = quad_tables()
    coef_rows = jnp.swapaxes(aero_coef, 1, 2)[offset_slot]
    kmask = jnp.where(contact_mask == 1, k_stick, jnp.where(contact_mask == 2, k_slip, 0.0)).astype(jnp.float32)
    old_rates = [evaluate(prev_nodes[j], stiffness, coef_rows, contact_left, contact_right, kmask) for j in range(4)]
    state = prev_nodes[0]
    rate = old_rates[0]
    for node_index in range(3):
        quad = old_rates[0] * float(table[node_index][0])
        for j in range(1, 4):
            quad = quad + float(table[node_index][j]) * old_rates[j]
        state = state + float(steps[node_index]) * (rate - old_rates[node_index]) + quad
        if node_index < 2:
            rate = evaluate(state, stiffness, coef_rows, contact_left, contact_right, kmask)
    growth = jnp.sqrt(jnp.mean(state * state) + 1e-06)
    return (state / growth, growth)
```

```python
import functools
import math

import jax
import jax.numpy as jnp
from jax import lax
from jax.experimental import pallas as pl
from jax.experimental.pallas import tpu as pltpu
from jax.sharding import PartitionSpec as P

DOF = 256
AERO = 128
TABLES = 32
LOCAL = 4
MESH = pl.DeviceIdType.MESH
F32 = jnp.float32
BF16 = jnp.bfloat16

time_step = 0.25
coupling = 0.5
damping = 0.1
k_stick = 4.0
k_slip = 1.0


def quad_tables():
    root = 1.0 / math.sqrt(5.0)
    tau = [0.0, (1.0 - root) / 2.0, (1.0 + root) / 2.0, 1.0]
    table = []
    for m in range(3):
        table_row = []
        for j in range(4):
            coeffs = [1.0]
            scale = 1.0
            for k in range(4):
                if k != j:
                    widened = [0.0] * (len(coeffs) + 1)
                    for power in range(len(coeffs)):
                        widened[power + 1] = widened[power + 1] + coeffs[power]
                        widened[power] = widened[power] - tau[k] * coeffs[power]
                    coeffs = widened
                    scale = scale * (tau[j] - tau[k])
            integral = 0.0
            for power in range(len(coeffs)):
                integral = integral + coeffs[power] * (
                    tau[m + 1] ** (power + 1) - tau[m] ** (power + 1)
                ) / (power + 1)
            table_row.append(integral / scale * time_step)
        table.append(table_row)
    steps = [(tau[m + 1] - tau[m]) * time_step for m in range(3)]
    return (table, steps)


S, H = quad_tables()
H1, H2 = H[1], H[2]
C1 = (1.0 - damping * H1) * (1.0 - damping * H2)
C2 = 1.0 - damping * H2
C3 = H1 + H2 * (1.0 - damping * H1)
HH = H1 * H2


def swap_halves(a, b):
    axis = a.ndim - 2
    low = lax.broadcasted_iota(jnp.int32, a.shape, axis) < 4
    return (
        jnp.where(low, a, pltpu.roll(b, 4, axis)),
        jnp.where(low, pltpu.roll(a, 4, axis), b),
    )


def low_of_pairs(rows):
    tiles = rows.reshape(rows.shape[0] // 16, 2, 8, 128)
    return swap_halves(tiles[:, 0], tiles[:, 1])[0]


def pairs_of_low(chunks):
    low = lax.broadcasted_iota(jnp.int32, chunks.shape, 1) < 4
    first = jnp.where(low, chunks, 0.0)
    second = jnp.where(low, pltpu.roll(chunks, 4, 1), 0.0)
    return jnp.stack([first, second], axis=1).reshape(chunks.shape[0] * 16, 128)


def dot(a, b, dims=(1, 0)):
    return lax.dot_general(
        a, b, (((dims[0],), (dims[1],)), ((), ())), preferred_element_type=F32
    )


def kernel(
    ns, nc, total_count,
    x_hbm, stiff_hbm, coef_hbm, slot_hbm, cl_hbm, cr_hbm, cm_hbm,
    out_hbm, growth_ref,
    xs, stiff, coef, slot, cl, cr, cm, cl_n, cr_n, cm_n,
    keff, mats, smat,
    yp0, yp1, yp2, a0r, halo, cross0, cross1, cross2,
    w_acc, p_acc, e1, e2p, e2w, st,
    send1, rcv1, send2, rcv2, send3, rcv3, send4, rcv4,
    nb_send, nb_rcv, acc1, acc2, part, colsum, secsum, secpart,
    load_sem, small_sem, out_sem,
    int_ssem, int_rsem, nb_ssem, nb_rsem, a_ssem, a_rsem, r_ssem, r_rsem,
):
    me = lax.axis_index("sector")
    mycol = lax.axis_index("col")
    rows = xs.shape[1]
    cols = 2 * ns
    sectors = LOCAL * ns
    block = min(64, rows)
    blocks = rows // block
    nxt = lax.rem(me + 1, ns)
    prv = lax.rem(me + ns - 1, ns)

    barrier = pltpu.get_barrier_semaphore()

    def greet_sector(i, carry):
        pl.semaphore_signal(
            barrier, inc=1, device_id={"sector": lax.rem(me + i, ns)}, device_id_type=MESH
        )
        return carry

    def greet_col(i, carry):
        pl.semaphore_signal(
            barrier, inc=1, device_id={"col": lax.rem(mycol + i, nc)}, device_id_type=MESH
        )
        return carry

    smalls = [
        pltpu.make_async_copy(src, dst, small_sem.at[n])
        for n, (src, dst) in enumerate(
            [(cl_hbm, cl), (cm_hbm, cm), (cr_hbm, cr), (slot_hbm, slot), (stiff_hbm, stiff)]
        )
    ]
    for copy in smalls:
        copy.start()
    loads = [pltpu.make_async_copy(x_hbm.at[n], xs.at[n], load_sem.at[n]) for n in range(8)]
    for copy in loads:
        copy.start()
    coef_load = pltpu.make_async_copy(coef_hbm, coef, load_sem.at[8])
    coef_load.start()
    lax.fori_loop(1, ns, greet_sector, 0)
    lax.fori_loop(1, nc, greet_col, 0)
    for copy in smalls:
        copy.wait()

    smat[...] = pltpu.roll(
        jnp.broadcast_to(slot[...].astype(F32), (sectors, sectors)), 0, 1, stride=1, stride_axis=0
    )

    pl.semaphore_wait(barrier, ns + nc - 2)

    int_copies = [
        pltpu.make_async_remote_copy(
            src, dst, int_ssem.at[n], int_rsem.at[n],
            device_id={"sector": to}, device_id_type=MESH,
        )
        for n, (src, dst, to) in enumerate([(cl, cl_n, nxt), (cm, cm_n, nxt), (cr, cr_n, prv)])
    ]
    for copy in int_copies:
        copy.start()

    for copy in loads:
        copy.wait()

    def combine(i, carry):
        at = pl.ds(pl.multiple_of(i * block, block), block)
        p = [xs[2 * j, at, :] for j in range(4)]
        w = [xs[2 * j + 1, at, :] for j in range(4)]

        def quad(m, v):
            out = v[0] * float(S[m][0])
            for j in range(1, 4):
                out = out + float(S[m][j]) * v[j]
            return out

        y0 = quad(0, p)
        v0 = quad(0, w)
        p1 = p[0] + v0
        y1 = quad(1, p) + H1 * (p1 - p[1])
        yp0[at, :] = y0
        yp1[at, :] = y1
        p_acc[at, :] = p1
        w_acc[at, :] = w[0] - damping * v0
        e1[at, :] = quad(1, w) - H1 * w[1]
        e2p[at, :] = quad(2, p) - H2 * p[2]
        e2w[at, :] = quad(2, w) - H2 * w[2]
        chunk = jnp.concatenate(
            [low_of_pairs(y0), low_of_pairs(C3 * y0 + H2 * y1)], axis=2
        ).astype(BF16)
        per = block // 16
        send1[pl.ds(i * per, per)] = chunk
        return carry

    lax.fori_loop(0, blocks, combine, 0)

    def sector_rows(ref, s):
        return jnp.concatenate(
            [ref[pl.ds(s, cols, stride=8), :], ref[pl.ds(4 + s, cols, stride=8), :]], axis=1
        ).astype(BF16)

    def neighbour_copies(field):
        return [
            pltpu.make_async_remote_copy(
                nb_send.at[side, field], nb_rcv.at[side, field],
                nb_ssem.at[side, field], nb_rsem.at[side, field],
                device_id={"sector": to}, device_id_type=MESH,
            )
            for side, to in ((0, prv), (1, nxt))
        ]

    def share_edges(field, ref):
        nb_send[0, field] = sector_rows(ref, 0)
        nb_send[1, field] = sector_rows(ref, LOCAL - 1)
        copies = neighbour_copies(field)
        for copy in copies:
            copy.start()
        return copies

    def send_all(src, dst, stage, ssem, rsem):
        def one(i, carry):
            to = lax.rem(me + i, ns)
            pltpu.make_async_remote_copy(
                src.at[to], dst.at[me], ssem.at[stage], rsem.at[stage],
                device_id={"sector": to}, device_id_type=MESH,
            ).start()
            return carry

        lax.fori_loop(1, ns, one, 0)
        dst[me] = src[me]

    def wait_all(src, dst, stage, ssem, rsem):
        most = pl.ds(0, ns - 1)
        return pltpu.make_async_remote_copy(
            src.at[most], dst.at[most], ssem.at[stage], rsem.at[stage],
            device_id={"sector": nxt}, device_id_type=MESH,
        )

    edge0 = share_edges(0, yp0)
    send_all(send1, rcv1, 0, a_ssem, a_rsem)
    edge1 = share_edges(1, yp1)

    for copy in int_copies:
        copy.wait()
    dof = lax.broadcasted_iota(jnp.int32, (DOF, 128), 0)
    mats_tri = jnp.where(
        jnp.abs(
            lax.broadcasted_iota(jnp.int32, (DOF, DOF), 0)
            - lax.broadcasted_iota(jnp.int32, (DOF, DOF), 1)
        )
        == 1,
        coupling,
        0.0,
    ).astype(BF16)
    diag = [None] * LOCAL
    for j in range(LOCAL + 1):
        left_ref, mask_ref, lrow = (cl_n, cm_n, LOCAL - 1) if j == 0 else (cl, cm, j - 1)
        right_ref, rrow = (cr_n, 0) if j == LOCAL else (cr, j)
        left = left_ref[pl.ds(lrow, 1), :]
        mask = mask_ref[pl.ds(lrow, 1), :]
        right = right_ref[pl.ds(rrow, 1), :]
        k = jnp.where(mask == 1, k_stick, jnp.where(mask == 2, k_slip, 0.0))
        at_left = jnp.where(dof == left, 1.0, 0.0).astype(BF16)
        at_right = jnp.where(dof == right, 1.0, 0.0).astype(BF16)
        k_left = jnp.where(dof == left, jnp.broadcast_to(k, (DOF, 128)), 0.0).astype(BF16)
        k8 = jnp.broadcast_to(k, (8, 128)).astype(BF16)
        if j > 0:
            mats[j - 1, 0:DOF, :] = dot(at_right, k_left, (1, 1)).astype(BF16)
            more = dot(k8, at_left, (1, 1))
            diag[j - 1] = more if diag[j - 1] is None else diag[j - 1] + more
        if j < LOCAL:
            mats[j, DOF:2 * DOF, :] = dot(k_left, at_right, (1, 1)).astype(BF16)
            mats[j, 2 * DOF:3 * DOF, :] = mats_tri
            diag[j] = dot(k8, at_right, (1, 1))
    row8 = lax.broadcasted_iota(jnp.int32, (8, 128), 0)
    total_k = stiff[...]
    for s in range(LOCAL):
        total_k = total_k + jnp.where(row8 == s, diag[s][:, 0:128], 0.0)
        total_k = total_k + jnp.where(row8 == LOCAL + s, diag[s][:, 128:256], 0.0)
    keff[...] = total_k

    def cross(own, next_first, prev_last, dst):
        chain = [prev_last] + own + [next_first]
        for s in range(LOCAL):
            lhs = jnp.concatenate([chain[s + 2], chain[s], chain[s + 1]], axis=1)
            out = dot(lhs, mats[s])
            dst[pl.ds(s, cols, stride=8), :] = out[:, 0:128]
            dst[pl.ds(4 + s, cols, stride=8), :] = out[:, 128:256]

    def cross_of(field, ref, dst):
        cross(
            [sector_rows(ref, s) for s in range(LOCAL)], nb_rcv[0, field], nb_rcv[1, field], dst
        )

    def times_k(rows_value):
        tiles = rows_value.reshape(rows_value.shape[0] // 8, 8, 128)
        return (tiles * keff[...][None]).reshape(rows_value.shape)

    for copy in edge0:
        copy.wait()
    cross_of(0, yp0, cross0)

    def second(i, carry):
        at = pl.ds(pl.multiple_of(i * block, block), block)
        y0 = yp0[at, :]
        w1 = w_acc[at, :] + cross0[at, :] - times_k(y0)
        v1 = H1 * w1 + e1[at, :]
        p2 = p_acc[at, :] + v1
        y2 = H2 * p2 + e2p[at, :]
        yp2[at, :] = y2
        p_acc[at, :] = p2
        w_acc[at, :] = w1 - damping * v1
        per = block // 16
        send2[pl.ds(i * per, per)] = low_of_pairs(C1 * y0 + C2 * yp1[at, :] + y2).astype(BF16)
        return carry

    lax.fori_loop(0, blocks, second, 0)
    send_all(send2, rcv2, 1, a_ssem, a_rsem)
    edge2 = share_edges(2, yp2)

    coef_load.wait()

    def loads_of(rhs, acc):
        width = rhs.shape[1] // AERO
        acc[...] = jnp.zeros_like(acc)

        def one(i, carry):
            pair = []
            tables = []
            for n in range(2):
                pick = jnp.where(smat[...] == (2 * i + n).astype(F32), 1.0, 0.0).astype(BF16)
                pair.append(dot(pick, rhs).astype(BF16))
                tables.append(coef[pl.ds(pl.multiple_of((2 * i + n) * AERO, AERO), AERO), :])
            lhs = jnp.concatenate(
                [
                    jnp.concatenate([g[:, c * AERO:(c + 1) * AERO] for g in pair], axis=1)
                    for c in range(width)
                ],
                axis=0,
            )
            acc[...] += dot(lhs, jnp.concatenate(tables, axis=1), (1, 1))
            return carry

        lax.fori_loop(0, TABLES // 2, one, 0)

    def by_sector(received):
        value = received.astype(F32).reshape(ns // 2, 2, 8, received.shape[2])
        first, second_ = swap_halves(value[:, 0], value[:, 1])
        return first.reshape(sectors, -1), second_.reshape(sectors, -1)

    def by_device(first, second_):
        lo, hi = swap_halves(
            first.reshape(ns // 2, 8, 128), second_.reshape(ns // 2, 8, 128)
        )
        return jnp.stack([lo, hi], axis=1).reshape(ns, 8, 128)

    wait_all(send1, rcv1, 0, a_ssem, a_rsem).wait()
    loads_of(jnp.concatenate(by_sector(rcv1[...]), axis=1).astype(BF16), acc1)
    a0 = [acc1[2 * c * sectors:(2 * c + 1) * sectors, :] for c in range(2)]
    b1 = [acc1[(2 * c + 1) * sectors:(2 * c + 2) * sectors, :] for c in range(2)]
    place = lax.broadcasted_iota(jnp.int32, (sectors, 128), 0) % LOCAL
    beside = [
        jnp.where(
            place == 0,
            pltpu.roll(a, 1, 0),
            jnp.where(place == LOCAL - 1, pltpu.roll(a, sectors - 1, 0), 0.0),
        )
        for a in a0
    ]
    send3[:, :, 0:128] = by_device(*a0).astype(BF16)
    send3[:, :, 128:256] = by_device(*beside).astype(BF16)
    send3[:, :, 256:384] = by_device(*b1).astype(BF16)
    send_all(send3, rcv3, 0, r_ssem, r_rsem)

    wait_all(send2, rcv2, 1, a_ssem, a_rsem).wait()
    rest = by_sector(rcv2[...])
    loads_of(
        jnp.concatenate(
            [rest[c] + HH * acc1[2 * c * sectors:(2 * c + 1) * sectors, :] for c in range(2)],
            axis=1,
        ).astype(BF16),
        acc2,
    )
    send4[...] = by_device(acc2[0:sectors, :], acc2[sectors:2 * sectors, :]).astype(BF16)
    send_all(send4, rcv4, 1, r_ssem, r_rsem)

    for copy in edge1 + edge2:
        copy.wait()
    cross_of(1, yp1, cross1)
    cross_of(2, yp2, cross2)

    def third(i, carry):
        at = pl.ds(pl.multiple_of(i * block, block), block)
        w2 = w_acc[at, :] + cross1[at, :] - times_k(yp1[at, :])
        v2 = H2 * w2 + e2w[at, :]
        p_acc[at, :] = p_acc[at, :] + v2
        w_acc[at, :] = w2 - damping * v2 + cross2[at, :] - times_k(yp2[at, :])
        return carry

    lax.fori_loop(0, blocks, third, 0)

    wait_all(send3, rcv3, 0, r_ssem, r_rsem).wait()

    def spread(i, carry):
        per = block // 16
        at = pl.ds(pl.multiple_of(i * block, block), block)
        got = rcv3[pl.ds(i * per, per)].astype(F32)
        a0r[at, :] = pairs_of_low(got[:, :, 0:128])
        halo[at, :] = pairs_of_low(got[:, :, 128:256])
        p3 = p_acc[at, :] + pairs_of_low(got[:, :, 256:384])
        st[0, at, :] = p3
        return carry + jnp.sum((p3 * p3).reshape(block // 8, 8, 128), axis=0)

    squares = lax.fori_loop(0, blocks, spread, jnp.zeros((8, 128), F32))
    out_p = pltpu.make_async_copy(st.at[0], out_hbm.at[0], out_sem.at[0])
    out_p.start()

    none = jnp.zeros((cols, 128), BF16)

    def surface_rows(ref, s):
        return jnp.concatenate([ref[pl.ds(s, cols, stride=8), :].astype(BF16), none], axis=1)

    cross(
        [surface_rows(a0r, s) for s in range(LOCAL)],
        surface_rows(halo, LOCAL - 1), surface_rows(halo, 0), cross0,
    )

    def fourth(i, carry):
        at = pl.ds(pl.multiple_of(i * block, block), block)
        w_acc[at, :] = w_acc[at, :] + HH * (cross0[at, :] - times_k(a0r[at, :]))
        return carry

    lax.fori_loop(0, blocks, fourth, 0)

    wait_all(send4, rcv4, 1, r_ssem, r_rsem).wait()

    def fifth(i, carry):
        per = block // 16
        at = pl.ds(pl.multiple_of(i * block, block), block)
        w3 = w_acc[at, :] + pairs_of_low(rcv4[pl.ds(i * per, per)].astype(F32))
        st[1, at, :] = w3
        return carry + jnp.sum((w3 * w3).reshape(block // 8, 8, 128), axis=0)

    squares = lax.fori_loop(0, blocks, fifth, squares)
    out_w = pltpu.make_async_copy(st.at[1], out_hbm.at[1], out_sem.at[1])
    out_w.start()

    part[...] = jnp.sum(squares, axis=0, keepdims=True)

    def to_col(i, carry):
        to = lax.rem(mycol + i, nc)
        pltpu.make_async_remote_copy(
            part, colsum.at[mycol], a_ssem.at[2], a_rsem.at[2],
            device_id={"col": to}, device_id_type=MESH,
        ).start()
        return carry

    lax.fori_loop(1, nc, to_col, 0)
    colsum[mycol] = part[...]
    most = pl.ds(0, nc - 1)
    pltpu.make_async_remote_copy(
        colsum.at[most], colsum.at[most], a_ssem.at[2], a_rsem.at[2],
        device_id={"sector": nxt}, device_id_type=MESH,
    ).wait()
    secpart[...] = jnp.sum(colsum[...], axis=0)

    def to_sector(i, carry):
        to = lax.rem(me + i, ns)
        pltpu.make_async_remote_copy(
            secpart, secsum.at[me], r_ssem.at[2], r_rsem.at[2],
            device_id={"sector": to}, device_id_type=MESH,
        ).start()
        return carry

    lax.fori_loop(1, ns, to_sector, 0)
    secsum[me] = secpart[...]
    wait_all(secsum, secsum, 2, r_ssem, r_rsem).wait()
    everything = jnp.sum(jnp.sum(secsum[...], axis=0), axis=1, keepdims=True)
    growth_ref[...] = jnp.broadcast_to(jnp.sqrt(everything / total_count + 1e-6), (1, 128))
    out_p.wait()
    out_w.wait()


def per_device(
    ns, nc, prev_nodes, stiffness, aero_coef, offset_slot, contact_left, contact_right, contact_mask
):
    cols = prev_nodes.shape[2]
    rows = cols * 8
    sectors = ns * LOCAL
    x = prev_nodes.reshape(8, cols, LOCAL, 2, 128).transpose(0, 1, 3, 2, 4).reshape(8, rows, 128)
    stiff = stiffness.reshape(LOCAL, 2, 128).transpose(1, 0, 2).reshape(8, 128)
    vm = pltpu.VMEM
    big = vm((rows, 128), F32)
    ints = vm((LOCAL, 128), jnp.int32)
    dma = pltpu.SemaphoreType.DMA
    any_spec = pl.BlockSpec(memory_space=pl.ANY)
    state, growth = pl.pallas_call(
        functools.partial(kernel, ns, nc, float(2 * cols * nc * sectors * DOF)),
        out_shape=(
            jax.ShapeDtypeStruct((2, rows, 128), F32),
            jax.ShapeDtypeStruct((1, 128), F32),
        ),
        in_specs=[any_spec] * 7,
        out_specs=(any_spec, pl.BlockSpec(memory_space=pltpu.VMEM)),
        scratch_shapes=[
            vm((8, rows, 128), F32),
            vm((8, 128), F32),
            vm((TABLES * AERO, AERO), BF16),
            vm((1, sectors), jnp.int32),
            ints, ints, ints, ints, ints, ints,
            vm((8, 128), F32),
            vm((LOCAL, 3 * DOF, DOF), BF16),
            vm((sectors, sectors), F32),
            big, big, big, big, big, big, big, big,
            big, big, big, big, big,
            vm((2, rows, 128), F32),
            vm((ns, 8, 256), BF16), vm((ns, 8, 256), BF16),
            vm((ns, 8, 128), BF16), vm((ns, 8, 128), BF16),
            vm((ns, 8, 384), BF16), vm((ns, 8, 384), BF16),
            vm((ns, 8, 128), BF16), vm((ns, 8, 128), BF16),
            vm((2, 3, cols, DOF), BF16), vm((2, 3, cols, DOF), BF16),
            vm((4 * sectors, AERO), F32),
            vm((2 * sectors, AERO), F32),
            vm((1, 128), F32),
            vm((nc, 1, 128), F32),
            vm((ns, 1, 128), F32),
            vm((1, 128), F32),
            dma((9,)), dma((5,)), dma((2,)),
            dma((3,)), dma((3,)), dma((2, 3)), dma((2, 3)),
            dma((3,)), dma((3,)), dma((3,)), dma((3,)),
        ],
        compiler_params=pltpu.CompilerParams(
            collective_id=0, has_side_effects=True, vmem_limit_bytes=60 << 20
        ),
        name="sweep",
    )(
        x, stiff, aero_coef.reshape(TABLES * AERO, AERO), offset_slot.reshape(1, sectors),
        contact_left, contact_right, contact_mask,
    )
    value = growth[0, 0]
    scaled = state / value
    scaled = scaled.reshape(2, cols, 2, LOCAL, 128).transpose(0, 1, 3, 2, 4)
    return scaled.reshape(2, cols, LOCAL, DOF), value


def solution(mesh):
    ns, nc = mesh.shape["sector"], mesh.shape["col"]
    placed = (
        P(None, None, "col", "sector", None),
        P("sector", None),
        P(),
        P(),
        P("sector", None),
        P("sector", None),
        P("sector", None),
    )
    return jax.shard_map(
        functools.partial(per_device, ns, nc),
        mesh=mesh,
        in_specs=placed,
        out_specs=(P(None, "col", "sector", None), P()),
        check_vma=False,
    )
```

```python
import functools
import math

import jax
import jax.numpy as jnp
from jax import lax
from jax.experimental import pallas as pl
from jax.experimental.pallas import tpu as pltpu
from jax.sharding import PartitionSpec as P

DOF = 256
AERO = 128
TABLES = 32
LOCAL = 4
MESH = pl.DeviceIdType.MESH
F32 = jnp.float32
BF16 = jnp.bfloat16

time_step = 0.25
coupling = 0.5
damping = 0.1
k_stick = 4.0
k_slip = 1.0


def quad_tables():
    root = 1.0 / math.sqrt(5.0)
    tau = [0.0, (1.0 - root) / 2.0, (1.0 + root) / 2.0, 1.0]
    table = []
    for m in range(3):
        table_row = []
        for j in range(4):
            coeffs = [1.0]
            scale = 1.0
            for k in range(4):
                if k != j:
                    widened = [0.0] * (len(coeffs) + 1)
                    for power in range(len(coeffs)):
                        widened[power + 1] = widened[power + 1] + coeffs[power]
                        widened[power] = widened[power] - tau[k] * coeffs[power]
                    coeffs = widened
                    scale = scale * (tau[j] - tau[k])
            integral = 0.0
            for power in range(len(coeffs)):
                integral = integral + coeffs[power] * (
                    tau[m + 1] ** (power + 1) - tau[m] ** (power + 1)
                ) / (power + 1)
            table_row.append(integral / scale * time_step)
        table.append(table_row)
    steps = [(tau[m + 1] - tau[m]) * time_step for m in range(3)]
    return (table, steps)


S, H = quad_tables()
H1, H2 = H[1], H[2]
C1 = (1.0 - damping * H1) * (1.0 - damping * H2)
C2 = 1.0 - damping * H2
C3 = H1 + H2 * (1.0 - damping * H1)
HH = H1 * H2


def swap_halves(a, b):
    axis = a.ndim - 2
    low = lax.broadcasted_iota(jnp.int32, a.shape, axis) < 4
    return (
        jnp.where(low, a, pltpu.roll(b, 4, axis)),
        jnp.where(low, pltpu.roll(a, 4, axis), b),
    )


def low_of_pairs(rows):
    tiles = rows.reshape(rows.shape[0] // 16, 2, 8, 128)
    return swap_halves(tiles[:, 0], tiles[:, 1])[0]


def pairs_of_low(chunks):
    low = lax.broadcasted_iota(jnp.int32, chunks.shape, 1) < 4
    first = jnp.where(low, chunks, 0.0)
    second = jnp.where(low, pltpu.roll(chunks, 4, 1), 0.0)
    return jnp.stack([first, second], axis=1).reshape(chunks.shape[0] * 16, 128)


def dot(a, b, dims=(1, 0)):
    return lax.dot_general(
        a, b, (((dims[0],), (dims[1],)), ((), ())), preferred_element_type=F32
    )


def kernel(
    ns, nc, total_count,
    x_hbm, stiff_hbm, coef_hbm, slot_hbm, cl_hbm, cr_hbm, cm_hbm,
    out_hbm, growth_ref,
    xs, stiff, coef, slot, cl, cr, cm, cl_n, cr_n, cm_n,
    keff, mats, picks, tabled,
    yp0, yp1, yp2, a0r, halo, cross0, cross1, cross2,
    w_acc, p_acc, e1, e2p, e2w, st,
    send1, rcv1, send2, rcv2, send3, rcv3, send4, rcv4,
    nb_send, nb_rcv, acc1, acc2, part, colsum, secsum, secpart,
    load_sem, small_sem, out_sem,
    int_ssem, int_rsem, nb_ssem, nb_rsem, a_ssem, a_rsem, r_ssem, r_rsem,
):
    me = lax.axis_index("sector")
    mycol = lax.axis_index("col")
    rows = xs.shape[1]
    cols = 2 * ns
    sectors = LOCAL * ns
    block = min(64, rows)
    blocks = rows // block
    nxt = lax.rem(me + 1, ns)
    prv = lax.rem(me + ns - 1, ns)

    barrier = pltpu.get_barrier_semaphore()

    def greet_sector(i, carry):
        pl.semaphore_signal(
            barrier, inc=1, device_id={"sector": lax.rem(me + i, ns)}, device_id_type=MESH
        )
        return carry

    def greet_col(i, carry):
        pl.semaphore_signal(
            barrier, inc=1, device_id={"col": lax.rem(mycol + i, nc)}, device_id_type=MESH
        )
        return carry

    loads = [pltpu.make_async_copy(x_hbm.at[n], xs.at[n], load_sem.at[n]) for n in range(8)]
    for copy in loads:
        copy.start()
    smalls = [
        pltpu.make_async_copy(src, dst, small_sem.at[n])
        for n, (src, dst) in enumerate(
            [(cl_hbm, cl), (cm_hbm, cm), (cr_hbm, cr), (slot_hbm, slot), (stiff_hbm, stiff)]
        )
    ]
    for copy in smalls:
        copy.start()
    for to in (prv, nxt):
        pl.semaphore_signal(barrier, inc=1, device_id={"sector": to}, device_id_type=MESH)
    lax.fori_loop(2, ns - 1, greet_sector, 0)
    lax.fori_loop(1, nc, greet_col, 0)
    coef_load = pltpu.make_async_copy(coef_hbm, coef, load_sem.at[8])
    coef_load.start()
    for copy in loads:
        copy.wait()

    def combine(i, carry):
        at = pl.ds(pl.multiple_of(i * block, block), block)
        p = [xs[2 * j, at, :] for j in range(4)]
        w = [xs[2 * j + 1, at, :] for j in range(4)]

        def quad(m, v):
            out = v[0] * float(S[m][0])
            for j in range(1, 4):
                out = out + float(S[m][j]) * v[j]
            return out

        y0 = quad(0, p)
        v0 = quad(0, w)
        p1 = p[0] + v0
        y1 = quad(1, p) + H1 * (p1 - p[1])
        yp0[at, :] = y0
        yp1[at, :] = y1
        p_acc[at, :] = p1
        w_acc[at, :] = w[0] - damping * v0
        e1[at, :] = quad(1, w) - H1 * w[1]
        e2p[at, :] = quad(2, p) - H2 * p[2]
        e2w[at, :] = quad(2, w) - H2 * w[2]
        chunk = jnp.concatenate(
            [low_of_pairs(y0), low_of_pairs(C3 * y0 + H2 * y1)], axis=2
        ).astype(BF16)
        per = block // 16
        send1[pl.ds(i * per, per)] = chunk
        return carry

    lax.fori_loop(0, blocks, combine, 0)

    def sector_rows(ref, s):
        return jnp.concatenate(
            [ref[pl.ds(s, cols, stride=8), :], ref[pl.ds(4 + s, cols, stride=8), :]], axis=1
        )

    def neighbour_copies(field):
        return [
            pltpu.make_async_remote_copy(
                nb_send.at[side, field], nb_rcv.at[side, field],
                nb_ssem.at[side, field], nb_rsem.at[side, field],
                device_id={"sector": to}, device_id_type=MESH,
            )
            for side, to in ((0, prv), (1, nxt))
        ]

    def fill_edges(field, ref):
        nb_send[0, field] = sector_rows(ref, 0).astype(BF16)
        nb_send[1, field] = sector_rows(ref, LOCAL - 1).astype(BF16)

    def send_all(src, dst, stage, ssem, rsem):
        def one(i, carry):
            to = lax.rem(me + i, ns)
            pltpu.make_async_remote_copy(
                src.at[to], dst.at[me], ssem.at[stage], rsem.at[stage],
                device_id={"sector": to}, device_id_type=MESH,
            ).start()
            return carry

        lax.fori_loop(1, ns, one, 0)
        dst[me] = src[me]

    def wait_all(src, dst, stage, ssem, rsem):
        most = pl.ds(0, ns - 1)
        return pltpu.make_async_remote_copy(
            src.at[most], dst.at[most], ssem.at[stage], rsem.at[stage],
            device_id={"sector": nxt}, device_id_type=MESH,
        )

    fill_edges(0, yp0)
    for copy in smalls:
        copy.wait()
    int_copies = [
        pltpu.make_async_remote_copy(
            src, dst, int_ssem.at[n], int_rsem.at[n],
            device_id={"sector": to}, device_id_type=MESH,
        )
        for n, (src, dst, to) in enumerate([(cl, cl_n, nxt), (cm, cm_n, nxt), (cr, cr_n, prv)])
    ]
    edge0, edge1, edge2 = [neighbour_copies(field) for field in range(3)]

    pl.semaphore_wait(barrier, ns + nc - 2)

    for copy in int_copies + edge0:
        copy.start()
    send_all(send1, rcv1, 0, a_ssem, a_rsem)
    fill_edges(1, yp1)
    for copy in edge1:
        copy.start()

    smat = pltpu.roll(
        jnp.broadcast_to(slot[...].astype(F32), (sectors, sectors)), 0, 1, stride=1, stride_axis=0
    )
    for k in range(TABLES):
        picks[:, k * sectors:(k + 1) * sectors] = jnp.where(smat == float(k), 1.0, 0.0).astype(BF16)

    for copy in int_copies:
        copy.wait()
    dof = lax.broadcasted_iota(jnp.int32, (DOF, 128), 0)
    mats_tri = jnp.where(
        jnp.abs(
            lax.broadcasted_iota(jnp.int32, (DOF, DOF), 0)
            - lax.broadcasted_iota(jnp.int32, (DOF, DOF), 1)
        )
        == 1,
        coupling,
        0.0,
    ).astype(BF16)
    diag = [None] * LOCAL
    for j in range(LOCAL + 1):
        left_ref, mask_ref, lrow = (cl_n, cm_n, LOCAL - 1) if j == 0 else (cl, cm, j - 1)
        right_ref, rrow = (cr_n, 0) if j == LOCAL else (cr, j)
        left = left_ref[pl.ds(lrow, 1), :]
        mask = mask_ref[pl.ds(lrow, 1), :]
        right = right_ref[pl.ds(rrow, 1), :]
        k = jnp.where(mask == 1, k_stick, jnp.where(mask == 2, k_slip, 0.0))
        at_left = jnp.where(dof == left, 1.0, 0.0).astype(BF16)
        at_right = jnp.where(dof == right, 1.0, 0.0).astype(BF16)
        k_left = jnp.where(dof == left, jnp.broadcast_to(k, (DOF, 128)), 0.0).astype(BF16)
        k8 = jnp.broadcast_to(k, (8, 128)).astype(BF16)
        if j > 0:
            mats[j - 1, 0:DOF, :] = dot(at_right, k_left, (1, 1)).astype(BF16)
            more = dot(k8, at_left, (1, 1))
            diag[j - 1] = more if diag[j - 1] is None else diag[j - 1] + more
        if j < LOCAL:
            mats[j, DOF:2 * DOF, :] = dot(k_left, at_right, (1, 1)).astype(BF16)
            mats[j, 2 * DOF:3 * DOF, :] = mats_tri
            diag[j] = dot(k8, at_right, (1, 1))
    row8 = lax.broadcasted_iota(jnp.int32, (8, 128), 0)
    total_k = stiff[...]
    for s in range(LOCAL):
        total_k = total_k + jnp.where(row8 == s, diag[s][:, 0:128], 0.0)
        total_k = total_k + jnp.where(row8 == LOCAL + s, diag[s][:, 128:256], 0.0)
    keff[...] = total_k

    def cross(own, next_first, prev_last, dst):
        chain = [prev_last] + own + [next_first]
        for s in range(LOCAL):
            lhs = jnp.concatenate([chain[s + 2], chain[s], chain[s + 1]], axis=1)
            out = dot(lhs, mats[s])
            dst[pl.ds(s, cols, stride=8), :] = out[:, 0:128]
            dst[pl.ds(4 + s, cols, stride=8), :] = out[:, 128:256]

    def cross_of(field, ref, dst):
        cross(
            [sector_rows(ref, s).astype(BF16) for s in range(LOCAL)],
            nb_rcv[0, field], nb_rcv[1, field], dst,
        )

    def fine_cross_of(field, ref, dst):
        none = jnp.zeros((cols, DOF), BF16)
        chain = [jnp.concatenate([nb_rcv[1, field], none], axis=0)]
        for s in range(LOCAL):
            value = sector_rows(ref, s)
            high = value.astype(BF16)
            chain.append(jnp.concatenate([high, (value - high.astype(F32)).astype(BF16)], axis=0))
        chain.append(jnp.concatenate([nb_rcv[0, field], none], axis=0))
        for s in range(LOCAL):
            both = dot(jnp.concatenate([chain[s + 2], chain[s], chain[s + 1]], axis=1), mats[s])
            out = both[0:cols] + both[cols:2 * cols]
            dst[pl.ds(s, cols, stride=8), :] = out[:, 0:128]
            dst[pl.ds(4 + s, cols, stride=8), :] = out[:, 128:256]

    def times_k(rows_value):
        tiles = rows_value.reshape(rows_value.shape[0] // 8, 8, 128)
        return (tiles * keff[...][None]).reshape(rows_value.shape)

    for copy in edge0:
        copy.wait()
    cross_of(0, yp0, cross0)

    def second(i, carry):
        at = pl.ds(pl.multiple_of(i * block, block), block)
        y0 = yp0[at, :]
        w1 = w_acc[at, :] + cross0[at, :] - times_k(y0)
        v1 = H1 * w1 + e1[at, :]
        p2 = p_acc[at, :] + v1
        y2 = H2 * p2 + e2p[at, :]
        yp2[at, :] = y2
        p_acc[at, :] = p2
        w_acc[at, :] = w1 - damping * v1
        per = block // 16
        send2[pl.ds(i * per, per)] = low_of_pairs(C1 * y0 + C2 * yp1[at, :] + y2).astype(BF16)
        return carry

    lax.fori_loop(0, blocks, second, 0)
    send_all(send2, rcv2, 1, a_ssem, a_rsem)
    fill_edges(2, yp2)
    for copy in edge2:
        copy.start()

    coef_load.wait()

    def loads_of(surfaces, acc):
        parts = len(surfaces)
        lhs = jnp.concatenate(surfaces, axis=0).astype(BF16)
        for k in range(0, TABLES, 2):
            u = dot(lhs, coef[k * AERO:(k + 2) * AERO, :], (1, 1)).astype(BF16)
            for n in range(2):
                for c in range(parts):
                    tabled[
                        (k + n) * sectors:(k + n + 1) * sectors, c * AERO:(c + 1) * AERO
                    ] = u[c * sectors:(c + 1) * sectors, n * AERO:(n + 1) * AERO]
        acc[...] = dot(picks[...], tabled[:, 0:parts * AERO])

    def by_sector(received):
        value = received.astype(F32).reshape(ns // 2, 2, 8, received.shape[2])
        first, second_ = swap_halves(value[:, 0], value[:, 1])
        return first.reshape(sectors, -1), second_.reshape(sectors, -1)

    def by_device(first, second_):
        lo, hi = swap_halves(
            first.reshape(ns // 2, 8, 128), second_.reshape(ns // 2, 8, 128)
        )
        return jnp.stack([lo, hi], axis=1).reshape(ns, 8, 128)

    wait_all(send1, rcv1, 0, a_ssem, a_rsem).wait()
    arrived = by_sector(rcv1[...])
    loads_of([arrived[c][:, f * AERO:(f + 1) * AERO] for c in range(2) for f in range(2)], acc1)
    a0 = [acc1[:, 2 * c * AERO:(2 * c + 1) * AERO] for c in range(2)]
    b1 = [acc1[:, (2 * c + 1) * AERO:(2 * c + 2) * AERO] for c in range(2)]
    place = lax.broadcasted_iota(jnp.int32, (sectors, 128), 0) % LOCAL
    beside = [
        jnp.where(
            place == 0,
            pltpu.roll(a, 1, 0),
            jnp.where(place == LOCAL - 1, pltpu.roll(a, sectors - 1, 0), 0.0),
        )
        for a in a0
    ]
    send3[:, :, 0:128] = by_device(*a0).astype(BF16)
    send3[:, :, 128:256] = by_device(*beside).astype(BF16)
    send3[:, :, 256:384] = by_device(*b1).astype(BF16)
    send_all(send3, rcv3, 0, r_ssem, r_rsem)

    for copy in edge1 + edge2:
        copy.wait()
    fine_cross_of(1, yp1, cross1)
    fine_cross_of(2, yp2, cross2)

    def third(i, carry):
        at = pl.ds(pl.multiple_of(i * block, block), block)
        w2 = w_acc[at, :] + cross1[at, :] - times_k(yp1[at, :])
        v2 = H2 * w2 + e2w[at, :]
        p_acc[at, :] = p_acc[at, :] + v2
        w_acc[at, :] = w2 - damping * v2 + cross2[at, :] - times_k(yp2[at, :])
        return carry

    lax.fori_loop(0, blocks, third, 0)

    wait_all(send2, rcv2, 1, a_ssem, a_rsem).wait()
    rest = by_sector(rcv2[...])
    loads_of(
        [rest[c] + HH * acc1[:, 2 * c * AERO:(2 * c + 1) * AERO] for c in range(2)], acc2
    )
    send4[...] = by_device(acc2[:, 0:AERO], acc2[:, AERO:2 * AERO])
    send_all(send4, rcv4, 1, r_ssem, r_rsem)

    wait_all(send3, rcv3, 0, r_ssem, r_rsem).wait()

    def spread(i, carry):
        per = block // 16
        at = pl.ds(pl.multiple_of(i * block, block), block)
        got = rcv3[pl.ds(i * per, per)].astype(F32)
        a0r[at, :] = pairs_of_low(got[:, :, 0:128])
        halo[at, :] = pairs_of_low(got[:, :, 128:256])
        p3 = p_acc[at, :] + pairs_of_low(got[:, :, 256:384])
        st[0, at, :] = p3
        return carry + jnp.sum((p3 * p3).reshape(block // 8, 8, 128), axis=0)

    squares = lax.fori_loop(0, blocks, spread, jnp.zeros((8, 128), F32))
    out_p = pltpu.make_async_copy(st.at[0], out_hbm.at[0], out_sem.at[0])
    out_p.start()

    none = jnp.zeros((cols, 128), BF16)

    def surface_rows(ref, s):
        return jnp.concatenate([ref[pl.ds(s, cols, stride=8), :].astype(BF16), none], axis=1)

    cross(
        [surface_rows(a0r, s) for s in range(LOCAL)],
        surface_rows(halo, LOCAL - 1), surface_rows(halo, 0), cross0,
    )

    def fourth(i, carry):
        at = pl.ds(pl.multiple_of(i * block, block), block)
        w_acc[at, :] = w_acc[at, :] + HH * (cross0[at, :] - times_k(a0r[at, :]))
        return carry

    lax.fori_loop(0, blocks, fourth, 0)

    wait_all(send4, rcv4, 1, r_ssem, r_rsem).wait()

    def fifth(i, carry):
        per = block // 16
        at = pl.ds(pl.multiple_of(i * block, block), block)
        w3 = w_acc[at, :] + pairs_of_low(rcv4[pl.ds(i * per, per)])
        st[1, at, :] = w3
        return carry + jnp.sum((w3 * w3).reshape(block // 8, 8, 128), axis=0)

    squares = lax.fori_loop(0, blocks, fifth, squares)
    out_w = pltpu.make_async_copy(st.at[1], out_hbm.at[1], out_sem.at[1])
    out_w.start()

    part[...] = jnp.sum(squares, axis=0, keepdims=True)

    def to_col(i, carry):
        to = lax.rem(mycol + i, nc)
        pltpu.make_async_remote_copy(
            part, colsum.at[mycol], a_ssem.at[2], a_rsem.at[2],
            device_id={"col": to}, device_id_type=MESH,
        ).start()
        return carry

    lax.fori_loop(1, nc, to_col, 0)
    colsum[mycol] = part[...]
    most = pl.ds(0, nc - 1)
    pltpu.make_async_remote_copy(
        colsum.at[most], colsum.at[most], a_ssem.at[2], a_rsem.at[2],
        device_id={"sector": nxt}, device_id_type=MESH,
    ).wait()
    secpart[...] = jnp.sum(colsum[...], axis=0)

    def to_sector(i, carry):
        to = lax.rem(me + i, ns)
        pltpu.make_async_remote_copy(
            secpart, secsum.at[me], r_ssem.at[2], r_rsem.at[2],
            device_id={"sector": to}, device_id_type=MESH,
        ).start()
        return carry

    lax.fori_loop(1, ns, to_sector, 0)
    secsum[me] = secpart[...]
    wait_all(secsum, secsum, 2, r_ssem, r_rsem).wait()
    everything = jnp.sum(jnp.sum(secsum[...], axis=0), axis=1, keepdims=True)
    growth_ref[...] = jnp.broadcast_to(jnp.sqrt(everything / total_count + 1e-6), (1, 128))
    out_p.wait()
    out_w.wait()


def per_device(
    ns, nc, prev_nodes, stiffness, aero_coef, offset_slot, contact_left, contact_right, contact_mask
):
    cols = prev_nodes.shape[2]
    rows = cols * 8
    sectors = ns * LOCAL
    x = prev_nodes.reshape(8, cols, LOCAL, 2, 128).transpose(0, 1, 3, 2, 4).reshape(8, rows, 128)
    stiff = stiffness.reshape(LOCAL, 2, 128).transpose(1, 0, 2).reshape(8, 128)
    vm = pltpu.VMEM
    big = vm((rows, 128), F32)
    ints = vm((LOCAL, 128), jnp.int32)
    dma = pltpu.SemaphoreType.DMA
    any_spec = pl.BlockSpec(memory_space=pl.ANY)
    state, growth = pl.pallas_call(
        functools.partial(kernel, ns, nc, float(2 * cols * nc * sectors * DOF)),
        out_shape=(
            jax.ShapeDtypeStruct((2, rows, 128), F32),
            jax.ShapeDtypeStruct((1, 128), F32),
        ),
        in_specs=[any_spec] * 7,
        out_specs=(any_spec, pl.BlockSpec(memory_space=pltpu.VMEM)),
        scratch_shapes=[
            vm((8, rows, 128), F32),
            vm((8, 128), F32),
            vm((TABLES * AERO, AERO), BF16),
            vm((1, sectors), jnp.int32),
            ints, ints, ints, ints, ints, ints,
            vm((8, 128), F32),
            vm((LOCAL, 3 * DOF, DOF), BF16),
            vm((sectors, TABLES * sectors), BF16),
            vm((TABLES * sectors, 4 * AERO), BF16),
            big, big, big, big, big, big, big, big,
            big, big, big, big, big,
            vm((2, rows, 128), F32),
            vm((ns, 8, 256), BF16), vm((ns, 8, 256), BF16),
            vm((ns, 8, 128), BF16), vm((ns, 8, 128), BF16),
            vm((ns, 8, 384), BF16), vm((ns, 8, 384), BF16),
            vm((ns, 8, 128), F32), vm((ns, 8, 128), F32),
            vm((2, 3, cols, DOF), BF16), vm((2, 3, cols, DOF), BF16),
            vm((sectors, 4 * AERO), F32),
            vm((sectors, 2 * AERO), F32),
            vm((1, 128), F32),
            vm((nc, 1, 128), F32),
            vm((ns, 1, 128), F32),
            vm((1, 128), F32),
            dma((9,)), dma((5,)), dma((2,)),
            dma((3,)), dma((3,)), dma((2, 3)), dma((2, 3)),
            dma((3,)), dma((3,)), dma((3,)), dma((3,)),
        ],
        compiler_params=pltpu.CompilerParams(
            collective_id=0, has_side_effects=True, vmem_limit_bytes=60 << 20
        ),
        name="sweep",
    )(
        x, stiff, aero_coef.reshape(TABLES * AERO, AERO), offset_slot.reshape(1, sectors),
        contact_left, contact_right, contact_mask,
    )
    value = growth[0, 0]
    scaled = state / value
    scaled = scaled.reshape(2, cols, 2, LOCAL, 128).transpose(0, 1, 3, 2, 4)
    return scaled.reshape(2, cols, LOCAL, DOF), value


def solution(mesh):
    ns, nc = mesh.shape["sector"], mesh.shape["col"]
    placed = (
        P(None, None, "col", "sector", None),
        P("sector", None),
        P(),
        P(),
        P("sector", None),
        P("sector", None),
        P("sector", None),
    )
    return jax.shard_map(
        functools.partial(per_device, ns, nc),
        mesh=mesh,
        in_specs=placed,
        out_specs=(P(None, "col", "sector", None), P()),
        check_vma=False,
    )
```

```python
import functools
import math

import jax
import jax.numpy as jnp
from jax import lax
from jax.experimental import pallas as pl
from jax.experimental.pallas import tpu as pltpu
from jax.sharding import PartitionSpec as P

DOF = 256
AERO = 128
TABLES = 32
LOCAL = 4
MESH = pl.DeviceIdType.MESH
F32 = jnp.float32
BF16 = jnp.bfloat16

time_step = 0.25
coupling = 0.5
damping = 0.1
k_stick = 4.0
k_slip = 1.0


def quad_tables():
    root = 1.0 / math.sqrt(5.0)
    tau = [0.0, (1.0 - root) / 2.0, (1.0 + root) / 2.0, 1.0]
    table = []
    for m in range(3):
        table_row = []
        for j in range(4):
            coeffs = [1.0]
            scale = 1.0
            for k in range(4):
                if k != j:
                    widened = [0.0] * (len(coeffs) + 1)
                    for power in range(len(coeffs)):
                        widened[power + 1] = widened[power + 1] + coeffs[power]
                        widened[power] = widened[power] - tau[k] * coeffs[power]
                    coeffs = widened
                    scale = scale * (tau[j] - tau[k])
            integral = 0.0
            for power in range(len(coeffs)):
                integral = integral + coeffs[power] * (
                    tau[m + 1] ** (power + 1) - tau[m] ** (power + 1)
                ) / (power + 1)
            table_row.append(integral / scale * time_step)
        table.append(table_row)
    steps = [(tau[m + 1] - tau[m]) * time_step for m in range(3)]
    return (table, steps)


S, H = quad_tables()
H1, H2 = H[1], H[2]
C1 = (1.0 - damping * H1) * (1.0 - damping * H2)
C2 = 1.0 - damping * H2
C3 = H1 + H2 * (1.0 - damping * H1)
HH = H1 * H2


def swap_halves(a, b):
    axis = a.ndim - 2
    low = lax.broadcasted_iota(jnp.int32, a.shape, axis) < 4
    return (
        jnp.where(low, a, pltpu.roll(b, 4, axis)),
        jnp.where(low, pltpu.roll(a, 4, axis), b),
    )


def low_of_pairs(rows):
    tiles = rows.reshape(rows.shape[0] // 16, 2, 8, 128)
    return swap_halves(tiles[:, 0], tiles[:, 1])[0]


def pairs_of_low(chunks):
    low = lax.broadcasted_iota(jnp.int32, chunks.shape, 1) < 4
    first = jnp.where(low, chunks, 0.0)
    second = jnp.where(low, pltpu.roll(chunks, 4, 1), 0.0)
    return jnp.stack([first, second], axis=1).reshape(chunks.shape[0] * 16, 128)


def dot(a, b, dims=(1, 0)):
    return lax.dot_general(
        a, b, (((dims[0],), (dims[1],)), ((), ())), preferred_element_type=F32
    )


def kernel(
    ns, nc, total_count,
    x_hbm, stiff_hbm, coef_hbm, slot_hbm, cl_hbm, cr_hbm, cm_hbm,
    st, growth_ref,
    xs, stiff, coef, slot, cl, cr, cm, cl_n, cr_n, cm_n,
    keff, mats, picks, tabled,
    yp0, yp1, yp2, a0r, cross0, cross1, cross2,
    w_acc, p_acc, e1, e2p, e2w,
    send1, rcv1, send2, rcv2, send3, rcv3, send4, rcv4, send5, rcv5,
    nb_send, nb_rcv, nb_low, nb_low_rcv, acc1, acc2, part, colsum, secsum, secpart,
    load_sem, small_sem,
    int_ssem, int_rsem, nb_ssem, nb_rsem, a_ssem, a_rsem, r_ssem, r_rsem,
    low_ssem, low_rsem,
):
    me = lax.axis_index("sector")
    mycol = lax.axis_index("col")
    rows = xs.shape[1]
    cols = 2 * ns
    sectors = LOCAL * ns
    block = min(64, rows // 4)
    blocks = rows // block
    nxt = lax.rem(me + 1, ns)
    prv = lax.rem(me + ns - 1, ns)

    barrier = pltpu.get_barrier_semaphore()

    def greet_sector(i, carry):
        pl.semaphore_signal(
            barrier, inc=1, device_id={"sector": lax.rem(me + i, ns)}, device_id_type=MESH
        )
        return carry

    def greet_other(i, carry):
        pl.semaphore_signal(
            barrier, inc=1,
            device_id={"sector": lax.rem(me + ns // 2, ns), "col": lax.rem(mycol + i, nc)},
            device_id_type=MESH,
        )
        return carry

    def greet_col(i, carry):
        pl.semaphore_signal(
            barrier, inc=1, device_id={"col": lax.rem(mycol + i, nc)}, device_id_type=MESH
        )
        return carry

    quarter = rows // 4
    loads = [
        pltpu.make_async_copy(
            x_hbm.at[:, pl.ds(n * quarter, quarter), :],
            xs.at[:, pl.ds(n * quarter, quarter), :],
            load_sem.at[n],
        )
        for n in range(4)
    ]
    for copy in loads:
        copy.start()
    smalls = [
        pltpu.make_async_copy(src, dst, small_sem.at[n])
        for n, (src, dst) in enumerate(
            [(cl_hbm, cl), (cm_hbm, cm), (cr_hbm, cr), (slot_hbm, slot), (stiff_hbm, stiff)]
        )
    ]
    for copy in smalls:
        copy.start()
    for to in (prv, nxt):
        pl.semaphore_signal(barrier, inc=1, device_id={"sector": to}, device_id_type=MESH)
    lax.fori_loop(2, ns - 1, greet_sector, 0)
    lax.fori_loop(1, nc, greet_col, 0)
    lax.fori_loop(1, nc, greet_other, 0)
    coef_load = pltpu.make_async_copy(coef_hbm, coef, load_sem.at[4])
    coef_load.start()
    def combine(i, carry):
        at = pl.ds(pl.multiple_of(i * block, block), block)
        p = [xs[2 * j, at, :] for j in range(4)]
        w = [xs[2 * j + 1, at, :] for j in range(4)]

        def quad(m, v):
            out = v[0] * float(S[m][0])
            for j in range(1, 4):
                out = out + float(S[m][j]) * v[j]
            return out

        y0 = quad(0, p)
        v0 = quad(0, w)
        p1 = p[0] + v0
        y1 = quad(1, p) + H1 * (p1 - p[1])
        yp0[at, :] = y0
        yp1[at, :] = y1
        p_acc[at, :] = p1
        w_acc[at, :] = w[0] - damping * v0
        e1[at, :] = quad(1, w) - H1 * w[1]
        e2p[at, :] = quad(2, p) - H2 * p[2]
        e2w[at, :] = quad(2, w) - H2 * w[2]
        chunk = jnp.concatenate(
            [low_of_pairs(y0), low_of_pairs(C3 * y0 + H2 * y1)], axis=2
        ).astype(BF16)
        per = block // 16
        send1[pl.ds(i * per, per)] = chunk
        return carry

    for n in range(4):
        loads[n].wait()
        lax.fori_loop(n * blocks // 4, (n + 1) * blocks // 4, combine, 0)

    def sector_rows(ref, s):
        return jnp.concatenate(
            [ref[pl.ds(s, cols, stride=8), :], ref[pl.ds(4 + s, cols, stride=8), :]], axis=1
        )

    def neighbour_copies(field):
        return [
            pltpu.make_async_remote_copy(
                nb_send.at[side, field], nb_rcv.at[side, field],
                nb_ssem.at[side, field], nb_rsem.at[side, field],
                device_id={"sector": to}, device_id_type=MESH,
            )
            for side, to in ((0, prv), (1, nxt))
        ]

    def fill_edges(field, ref):
        nb_send[0, field] = sector_rows(ref, 0).astype(BF16)
        nb_send[1, field] = sector_rows(ref, LOCAL - 1).astype(BF16)

    def send_all(src, dst, stage, ssem, rsem):
        def one(i, carry):
            to = lax.rem(me + i, ns)
            pltpu.make_async_remote_copy(
                src.at[to], dst.at[me], ssem.at[stage], rsem.at[stage],
                device_id={"sector": to}, device_id_type=MESH,
            ).start()
            return carry

        lax.fori_loop(1, ns, one, 0)
        dst[me] = src[me]

    def wait_all(src, dst, stage, ssem, rsem):
        most = pl.ds(0, ns - 1)
        return pltpu.make_async_remote_copy(
            src.at[most], dst.at[most], ssem.at[stage], rsem.at[stage],
            device_id={"sector": nxt}, device_id_type=MESH,
        )

    fill_edges(0, yp0)
    for copy in smalls:
        copy.wait()
    int_copies = [
        pltpu.make_async_remote_copy(
            src, dst, int_ssem.at[n], int_rsem.at[n],
            device_id={"sector": to}, device_id_type=MESH,
        )
        for n, (src, dst, to) in enumerate([(cl, cl_n, nxt), (cm, cm_n, nxt), (cr, cr_n, prv)])
    ]
    edge0, edge1, edge2 = [neighbour_copies(field) for field in range(3)]

    pl.semaphore_wait(barrier, ns + 2 * nc - 3)

    for copy in int_copies + edge0:
        copy.start()
    send_all(send1, rcv1, 0, a_ssem, a_rsem)
    fill_edges(1, yp1)
    for copy in edge1:
        copy.start()

    smat = pltpu.roll(
        jnp.broadcast_to(slot[...].astype(F32), (sectors, sectors)), 0, 1, stride=1, stride_axis=0
    )
    for k in range(TABLES):
        picks[:, k * sectors:(k + 1) * sectors] = jnp.where(smat == float(k), 1.0, 0.0).astype(BF16)

    for copy in int_copies:
        copy.wait()
    dof = lax.broadcasted_iota(jnp.int32, (DOF, 128), 0)
    mats_tri = jnp.where(
        jnp.abs(
            lax.broadcasted_iota(jnp.int32, (DOF, DOF), 0)
            - lax.broadcasted_iota(jnp.int32, (DOF, DOF), 1)
        )
        == 1,
        coupling,
        0.0,
    ).astype(BF16)
    diag = [None] * LOCAL
    for j in range(LOCAL + 1):
        left_ref, mask_ref, lrow = (cl_n, cm_n, LOCAL - 1) if j == 0 else (cl, cm, j - 1)
        right_ref, rrow = (cr_n, 0) if j == LOCAL else (cr, j)
        left = left_ref[pl.ds(lrow, 1), :]
        mask = mask_ref[pl.ds(lrow, 1), :]
        right = right_ref[pl.ds(rrow, 1), :]
        k = jnp.where(mask == 1, k_stick, jnp.where(mask == 2, k_slip, 0.0))
        at_left = jnp.where(dof == left, 1.0, 0.0).astype(BF16)
        at_right = jnp.where(dof == right, 1.0, 0.0).astype(BF16)
        k_left = jnp.where(dof == left, jnp.broadcast_to(k, (DOF, 128)), 0.0).astype(BF16)
        k8 = jnp.broadcast_to(k, (8, 128)).astype(BF16)
        if j > 0:
            mats[j - 1, 0:DOF, :] = dot(at_right, k_left, (1, 1)).astype(BF16)
            more = dot(k8, at_left, (1, 1))
            diag[j - 1] = more if diag[j - 1] is None else diag[j - 1] + more
        if j < LOCAL:
            mats[j, DOF:2 * DOF, :] = dot(k_left, at_right, (1, 1)).astype(BF16)
            mats[j, 2 * DOF:3 * DOF, :] = mats_tri
            diag[j] = dot(k8, at_right, (1, 1))
    row8 = lax.broadcasted_iota(jnp.int32, (8, 128), 0)
    total_k = stiff[...]
    for s in range(LOCAL):
        total_k = total_k + jnp.where(row8 == s, diag[s][:, 0:128], 0.0)
        total_k = total_k + jnp.where(row8 == LOCAL + s, diag[s][:, 128:256], 0.0)
    keff[...] = total_k

    def cross(own, next_first, prev_last, dst):
        chain = [prev_last] + own + [next_first]
        for s in range(LOCAL):
            lhs = jnp.concatenate([chain[s + 2], chain[s], chain[s + 1]], axis=1)
            out = dot(lhs, mats[s])
            dst[pl.ds(s, cols, stride=8), :] = out[:, 0:128]
            dst[pl.ds(4 + s, cols, stride=8), :] = out[:, 128:256]

    def cross_of(field, ref, dst):
        cross(
            [sector_rows(ref, s).astype(BF16) for s in range(LOCAL)],
            nb_rcv[0, field], nb_rcv[1, field], dst,
        )

    def fine_cross_of(field, ref, dst):
        none = jnp.zeros((cols, DOF), BF16)
        chain = [jnp.concatenate([nb_rcv[1, field], none], axis=0)]
        for s in range(LOCAL):
            value = sector_rows(ref, s)
            high = value.astype(BF16)
            chain.append(jnp.concatenate([high, (value - high.astype(F32)).astype(BF16)], axis=0))
        chain.append(jnp.concatenate([nb_rcv[0, field], none], axis=0))
        for s in range(LOCAL):
            both = dot(jnp.concatenate([chain[s + 2], chain[s], chain[s + 1]], axis=1), mats[s])
            out = both[0:cols] + both[cols:2 * cols]
            dst[pl.ds(s, cols, stride=8), :] = out[:, 0:128]
            dst[pl.ds(4 + s, cols, stride=8), :] = out[:, 128:256]

    def times_k(rows_value):
        tiles = rows_value.reshape(rows_value.shape[0] // 8, 8, 128)
        return (tiles * keff[...][None]).reshape(rows_value.shape)

    for copy in edge0:
        copy.wait()
    cross_of(0, yp0, cross0)

    def second(i, carry):
        at = pl.ds(pl.multiple_of(i * block, block), block)
        y0 = yp0[at, :]
        w1 = w_acc[at, :] + cross0[at, :] - times_k(y0)
        v1 = H1 * w1 + e1[at, :]
        p2 = p_acc[at, :] + v1
        y2 = H2 * p2 + e2p[at, :]
        yp2[at, :] = y2
        p_acc[at, :] = p2
        w_acc[at, :] = w1 - damping * v1
        per = block // 16
        send2[pl.ds(i * per, per)] = low_of_pairs(C1 * y0 + C2 * yp1[at, :] + y2).astype(BF16)
        return carry

    lax.fori_loop(0, blocks, second, 0)
    send_all(send2, rcv2, 1, a_ssem, a_rsem)
    fill_edges(2, yp2)
    for copy in edge2:
        copy.start()

    coef_load.wait()

    def loads_of(surfaces, acc):
        parts = len(surfaces)
        lhs = jnp.concatenate(surfaces, axis=0).astype(BF16)
        for k in range(0, TABLES, 2):
            u = dot(lhs, coef[k * AERO:(k + 2) * AERO, :], (1, 1)).astype(BF16)
            for n in range(2):
                for c in range(parts):
                    tabled[
                        (k + n) * sectors:(k + n + 1) * sectors, c * AERO:(c + 1) * AERO
                    ] = u[c * sectors:(c + 1) * sectors, n * AERO:(n + 1) * AERO]
        acc[...] = dot(picks[...], tabled[:, 0:parts * AERO])

    def by_sector(received):
        value = received.astype(F32).reshape(ns // 2, 2, 8, received.shape[2])
        first, second_ = swap_halves(value[:, 0], value[:, 1])
        return first.reshape(sectors, -1), second_.reshape(sectors, -1)

    def by_device(first, second_):
        lo, hi = swap_halves(
            first.reshape(ns // 2, 8, 128), second_.reshape(ns // 2, 8, 128)
        )
        return jnp.stack([lo, hi], axis=1).reshape(ns, 8, 128)

    wait_all(send1, rcv1, 0, a_ssem, a_rsem).wait()
    arrived = by_sector(rcv1[...])
    loads_of([arrived[c][:, 0:AERO] for c in range(2)], acc1)
    send3[...] = by_device(acc1[:, 0:AERO], acc1[:, AERO:2 * AERO]).astype(BF16)
    send_all(send3, rcv3, 0, r_ssem, r_rsem)
    loads_of([arrived[c][:, AERO:2 * AERO] for c in range(2)], acc2)
    send5[...] = by_device(acc2[:, 0:AERO], acc2[:, AERO:2 * AERO]).astype(BF16)
    send_all(send5, rcv5, 3, r_ssem, r_rsem)

    for copy in edge1 + edge2:
        copy.wait()
    fine_cross_of(1, yp1, cross1)
    fine_cross_of(2, yp2, cross2)

    def third(i, carry):
        at = pl.ds(pl.multiple_of(i * block, block), block)
        w2 = w_acc[at, :] + cross1[at, :] - times_k(yp1[at, :])
        v2 = H2 * w2 + e2w[at, :]
        p_acc[at, :] = p_acc[at, :] + v2
        w_acc[at, :] = w2 - damping * v2 + cross2[at, :] - times_k(yp2[at, :])
        return carry

    lax.fori_loop(0, blocks, third, 0)

    wait_all(send2, rcv2, 1, a_ssem, a_rsem).wait()
    rest = by_sector(rcv2[...])
    loads_of(
        [rest[c] + HH * acc1[:, c * AERO:(c + 1) * AERO] for c in range(2)], acc2
    )
    send4[...] = by_device(acc2[:, 0:AERO], acc2[:, AERO:2 * AERO]).astype(BF16)
    send_all(send4, rcv4, 1, r_ssem, r_rsem)

    wait_all(send3, rcv3, 0, r_ssem, r_rsem).wait()

    def spread(i, carry):
        per = block // 16
        at = pl.ds(pl.multiple_of(i * block, block), block)
        a0r[at, :] = pairs_of_low(rcv3[pl.ds(i * per, per)].astype(F32))
        return carry

    lax.fori_loop(0, blocks, spread, 0)

    none = jnp.zeros((cols, 128), BF16)
    own = [a0r[pl.ds(s, cols, stride=8), :].astype(BF16) for s in range(LOCAL)]
    nb_low[0] = own[0]
    nb_low[1] = own[LOCAL - 1]
    edge_low = [
        pltpu.make_async_remote_copy(
            nb_low.at[side], nb_low_rcv.at[side], low_ssem.at[side], low_rsem.at[side],
            device_id={"sector": to}, device_id_type=MESH,
        )
        for side, to in ((0, prv), (1, nxt))
    ]
    for copy in edge_low:
        copy.start()

    wait_all(send5, rcv5, 3, r_ssem, r_rsem).wait()

    def close_p(i, carry):
        per = block // 16
        at = pl.ds(pl.multiple_of(i * block, block), block)
        p3 = p_acc[at, :] + pairs_of_low(rcv5[pl.ds(i * per, per)].astype(F32))
        st[0, at, :] = p3
        return carry + jnp.sum((p3 * p3).reshape(block // 8, 8, 128), axis=0)

    squares = lax.fori_loop(0, blocks, close_p, jnp.zeros((8, 128), F32))

    for copy in edge_low:
        copy.wait()
    cross(
        [jnp.concatenate([v, none], axis=1) for v in own],
        jnp.concatenate([nb_low_rcv[0], none], axis=1),
        jnp.concatenate([nb_low_rcv[1], none], axis=1),
        cross0,
    )

    def fourth(i, carry):
        at = pl.ds(pl.multiple_of(i * block, block), block)
        w_acc[at, :] = w_acc[at, :] + HH * (cross0[at, :] - times_k(a0r[at, :]))
        return carry

    lax.fori_loop(0, blocks, fourth, 0)

    wait_all(send4, rcv4, 1, r_ssem, r_rsem).wait()

    def fifth(i, carry):
        per = block // 16
        at = pl.ds(pl.multiple_of(i * block, block), block)
        w3 = w_acc[at, :] + pairs_of_low(rcv4[pl.ds(i * per, per)].astype(F32))
        st[1, at, :] = w3
        return carry + jnp.sum((w3 * w3).reshape(block // 8, 8, 128), axis=0)

    squares = lax.fori_loop(0, blocks, fifth, squares)

    part[...] = jnp.sum(squares, axis=0, keepdims=True)

    half = ns // 2
    low, high = lax.rem(me, half), me // half
    spot = high * nc + mycol

    def over_high(i, carry):
        to = lax.rem(spot + i, 2 * nc)
        pltpu.make_async_remote_copy(
            part, colsum.at[spot], a_ssem.at[2], a_rsem.at[2],
            device_id={"sector": low + half * (to // nc), "col": lax.rem(to, nc)},
            device_id_type=MESH,
        ).start()
        return carry

    lax.fori_loop(1, 2 * nc, over_high, 0)
    colsum[spot] = part[...]
    most = pl.ds(0, 2 * nc - 1)
    pltpu.make_async_remote_copy(
        colsum.at[most], colsum.at[most], a_ssem.at[2], a_rsem.at[2],
        device_id={"sector": nxt}, device_id_type=MESH,
    ).wait()
    secpart[...] = jnp.sum(colsum[...], axis=0)

    def over_low(i, carry):
        to = lax.rem(low + i, half)
        pltpu.make_async_remote_copy(
            secpart, secsum.at[low], r_ssem.at[2], r_rsem.at[2],
            device_id={"sector": high * half + to}, device_id_type=MESH,
        ).start()
        return carry

    lax.fori_loop(1, half, over_low, 0)
    secsum[low] = secpart[...]
    most_low = pl.ds(0, half - 1)
    pltpu.make_async_remote_copy(
        secsum.at[most_low], secsum.at[most_low], r_ssem.at[2], r_rsem.at[2],
        device_id={"sector": nxt}, device_id_type=MESH,
    ).wait()
    everything = jnp.sum(jnp.sum(secsum[...], axis=0), axis=1, keepdims=True)
    growth_ref[...] = jnp.broadcast_to(jnp.sqrt(everything / total_count + 1e-6), (1, 128))


def per_device(
    ns, nc, prev_nodes, stiffness, aero_coef, offset_slot, contact_left, contact_right, contact_mask
):
    cols = prev_nodes.shape[2]
    rows = cols * 8
    sectors = ns * LOCAL
    x = prev_nodes.reshape(8, cols, LOCAL, 2, 128).transpose(0, 1, 3, 2, 4).reshape(8, rows, 128)
    stiff = stiffness.reshape(LOCAL, 2, 128).transpose(1, 0, 2).reshape(8, 128)
    vm = pltpu.VMEM
    big = vm((rows, 128), F32)
    ints = vm((LOCAL, 128), jnp.int32)
    dma = pltpu.SemaphoreType.DMA
    any_spec = pl.BlockSpec(memory_space=pl.ANY)
    state, growth = pl.pallas_call(
        functools.partial(kernel, ns, nc, float(2 * cols * nc * sectors * DOF)),
        out_shape=(
            pltpu.VMEM((2, rows, 128), F32),
            pltpu.VMEM((1, 128), F32),
        ),
        in_specs=[any_spec] * 7,
        out_specs=(pl.BlockSpec(memory_space=pltpu.VMEM), pl.BlockSpec(memory_space=pltpu.VMEM)),
        scratch_shapes=[
            vm((8, rows, 128), F32),
            vm((8, 128), F32),
            vm((TABLES * AERO, AERO), BF16),
            vm((1, sectors), jnp.int32),
            ints, ints, ints, ints, ints, ints,
            vm((8, 128), F32),
            vm((LOCAL, 3 * DOF, DOF), BF16),
            vm((sectors, TABLES * sectors), BF16),
            vm((TABLES * sectors, 2 * AERO), BF16),
            big, big, big, big, big, big, big,
            big, big, big, big, big,
            vm((ns, 8, 256), BF16), vm((ns, 8, 256), BF16),
            vm((ns, 8, 128), BF16), vm((ns, 8, 128), BF16),
            vm((ns, 8, 128), BF16), vm((ns, 8, 128), BF16),
            vm((ns, 8, 128), BF16), vm((ns, 8, 128), BF16),
            vm((ns, 8, 128), BF16), vm((ns, 8, 128), BF16),
            vm((2, 3, cols, DOF), BF16), vm((2, 3, cols, DOF), BF16),
            vm((2, cols, 128), BF16), vm((2, cols, 128), BF16),
            vm((sectors, 2 * AERO), F32),
            vm((sectors, 2 * AERO), F32),
            vm((1, 128), F32),
            vm((2 * nc, 1, 128), F32),
            vm((ns // 2, 1, 128), F32),
            vm((1, 128), F32),
            dma((5,)), dma((5,)),
            dma((3,)), dma((3,)), dma((2, 3)), dma((2, 3)),
            dma((3,)), dma((3,)), dma((4,)), dma((4,)),
            dma((2,)), dma((2,)),
        ],
        compiler_params=pltpu.CompilerParams(
            collective_id=0, has_side_effects=True, vmem_limit_bytes=60 << 20
        ),
        name="sweep",
    )(
        x, stiff, aero_coef.reshape(TABLES * AERO, AERO), offset_slot.reshape(1, sectors),
        contact_left, contact_right, contact_mask,
    )
    value = growth[0, 0]
    scaled = state / value
    scaled = scaled.reshape(2, cols, 2, LOCAL, 128).transpose(0, 1, 3, 2, 4)
    return scaled.reshape(2, cols, LOCAL, DOF), value


def solution(mesh):
    ns, nc = mesh.shape["sector"], mesh.shape["col"]
    placed = (
        P(None, None, "col", "sector", None),
        P("sector", None),
        P(),
        P(),
        P("sector", None),
        P("sector", None),
        P("sector", None),
    )
    return jax.shard_map(
        functools.partial(per_device, ns, nc),
        mesh=mesh,
        in_specs=placed,
        out_specs=(P(None, "col", "sector", None), P()),
        check_vma=False,
    )
```

```python
import functools
import math

import jax
import jax.numpy as jnp
from jax import lax
from jax.experimental import pallas as pl
from jax.experimental.pallas import tpu as pltpu
from jax.sharding import PartitionSpec as P

DOF = 256
AERO = 128
TABLES = 32
LOCAL = 4
MESH = pl.DeviceIdType.MESH
F32 = jnp.float32
BF16 = jnp.bfloat16

time_step = 0.25
coupling = 0.5
damping = 0.1
k_stick = 4.0
k_slip = 1.0


def quad_tables():
    root = 1.0 / math.sqrt(5.0)
    tau = [0.0, (1.0 - root) / 2.0, (1.0 + root) / 2.0, 1.0]
    table = []
    for m in range(3):
        table_row = []
        for j in range(4):
            coeffs = [1.0]
            scale = 1.0
            for k in range(4):
                if k != j:
                    widened = [0.0] * (len(coeffs) + 1)
                    for power in range(len(coeffs)):
                        widened[power + 1] = widened[power + 1] + coeffs[power]
                        widened[power] = widened[power] - tau[k] * coeffs[power]
                    coeffs = widened
                    scale = scale * (tau[j] - tau[k])
            integral = 0.0
            for power in range(len(coeffs)):
                integral = integral + coeffs[power] * (
                    tau[m + 1] ** (power + 1) - tau[m] ** (power + 1)
                ) / (power + 1)
            table_row.append(integral / scale * time_step)
        table.append(table_row)
    steps = [(tau[m + 1] - tau[m]) * time_step for m in range(3)]
    return (table, steps)


S, H = quad_tables()
H1, H2 = H[1], H[2]
C1 = (1.0 - damping * H1) * (1.0 - damping * H2)
C2 = 1.0 - damping * H2
C3 = H1 + H2 * (1.0 - damping * H1)
HH = H1 * H2


def swap_halves(a, b):
    axis = a.ndim - 2
    low = lax.broadcasted_iota(jnp.int32, a.shape, axis) < 4
    return (
        jnp.where(low, a, pltpu.roll(b, 4, axis)),
        jnp.where(low, pltpu.roll(a, 4, axis), b),
    )


def low_of_pairs(rows):
    tiles = rows.reshape(rows.shape[0] // 16, 2, 8, 128)
    return swap_halves(tiles[:, 0], tiles[:, 1])[0]


def pairs_of_low(chunks):
    low = lax.broadcasted_iota(jnp.int32, chunks.shape, 1) < 4
    first = jnp.where(low, chunks, 0.0)
    second = jnp.where(low, pltpu.roll(chunks, 4, 1), 0.0)
    return jnp.stack([first, second], axis=1).reshape(chunks.shape[0] * 16, 128)


def far_first(step, length):
    return lax.rem(length // 2 + length + (1 - 2 * lax.rem(step, 2)) * ((step + 1) // 2), length)


def dot(a, b, dims=(1, 0)):
    return lax.dot_general(
        a, b, (((dims[0],), (dims[1],)), ((), ())), preferred_element_type=F32
    )


def kernel(
    ns, nc, total_count,
    x_hbm, stiff_hbm, coef_hbm, slot_hbm, cl_hbm, cr_hbm, cm_hbm,
    st, growth_ref,
    xs, stiff, coef, slot, cl, cr, cm,
    keff, mats, ends, picks, tabled,
    yp0, yp1, yp2, a0r, cross0, cross1, cross2,
    w_acc, p_acc, e1, e2p, e2w,
    send1, rcv1, send2, rcv2, send3, rcv3, send4, rcv4, send5, rcv5,
    nb_send, nb_rcv, nb_low, nb_low_rcv, acc1, acc2, part, colsum, secsum, secpart,
    load_sem, small_sem,
    nb_ssem, nb_rsem, a_ssem, a_rsem, r_ssem, r_rsem,
    low_ssem, low_rsem,
):
    me = lax.axis_index("sector")
    mycol = lax.axis_index("col")
    rows = xs.shape[1]
    cols = 2 * ns
    sectors = LOCAL * ns
    block = min(64, rows // 4)
    blocks = rows // block
    nxt = lax.rem(me + 1, ns)
    prv = lax.rem(me + ns - 1, ns)

    barrier = pltpu.get_barrier_semaphore()

    rings = ns // 4
    half = ns // 2
    wide = nc // 2
    core, along, high = lax.rem(me, 2), lax.rem(me // 2, rings), me // half
    across, lane = mycol // 2, lax.rem(mycol, 2)

    def peer(i):
        step, rest = far_first(i // 4, rings), lax.rem(i, 4)
        return (
            lax.rem(high + 1 - rest // 2, 2) * half
            + lax.rem(along + step, rings) * 2
            + lax.rem(core + 1 - lax.rem(rest, 2), 2)
        )

    def low_peer(i):
        step = far_first(i // 2, rings)
        return lax.rem(along + step, rings) * 2 + lax.rem(core + 1 - lax.rem(i, 2), 2)

    def high_peer(i):
        step, rest = far_first(i // 4, wide), lax.rem(i, 4)
        to = lax.rem(across + step, wide) * 2 + lax.rem(lane + 1 - lax.rem(rest, 2), 2)
        return lax.rem(high + 1 - rest // 2, 2), to

    def greet_sector(i, carry):
        pl.semaphore_signal(
            barrier, inc=1, device_id={"sector": peer(i)}, device_id_type=MESH
        )
        return carry

    def greet_other(i, carry):
        pl.semaphore_signal(
            barrier, inc=1,
            device_id={"sector": lax.rem(me + ns // 2, ns), "col": lax.rem(mycol + i, nc)},
            device_id_type=MESH,
        )
        return carry

    def greet_col(i, carry):
        pl.semaphore_signal(
            barrier, inc=1, device_id={"col": lax.rem(mycol + i, nc)}, device_id_type=MESH
        )
        return carry

    quarter = rows // 4
    loads = [
        pltpu.make_async_copy(
            x_hbm.at[:, pl.ds(n * quarter, quarter), :],
            xs.at[:, pl.ds(n * quarter, quarter), :],
            load_sem.at[n],
        )
        for n in range(4)
    ]
    for copy in loads:
        copy.start()
    lax.fori_loop(0, ns - 1, greet_sector, 0)
    lax.fori_loop(1, nc, greet_other, 0)
    lax.fori_loop(1, nc, greet_col, 0)
    smalls = [
        pltpu.make_async_copy(src, dst, small_sem.at[n])
        for n, (src, dst) in enumerate(
            [(cl_hbm, cl), (cm_hbm, cm), (cr_hbm, cr), (stiff_hbm, stiff), (slot_hbm, slot)]
        )
    ]
    for copy in smalls:
        copy.start()
    coef_load = pltpu.make_async_copy(coef_hbm, coef, load_sem.at[4])
    coef_load.start()

    def combine(i, carry):
        at = pl.ds(pl.multiple_of(i * block, block), block)
        p = [xs[2 * j, at, :] for j in range(4)]
        w = [xs[2 * j + 1, at, :] for j in range(4)]

        def quad(m, v):
            out = v[0] * float(S[m][0])
            for j in range(1, 4):
                out = out + float(S[m][j]) * v[j]
            return out

        y0 = quad(0, p)
        v0 = quad(0, w)
        p1 = p[0] + v0
        y1 = quad(1, p) + H1 * (p1 - p[1])
        yp0[at, :] = y0
        yp1[at, :] = y1
        p_acc[at, :] = p1
        w_acc[at, :] = w[0] - damping * v0
        e1[at, :] = quad(1, w) - H1 * w[1]
        e2p[at, :] = quad(2, p) - H2 * p[2]
        e2w[at, :] = quad(2, w) - H2 * w[2]
        chunk = jnp.concatenate(
            [low_of_pairs(y0), low_of_pairs(C3 * y0 + H2 * y1)], axis=2
        ).astype(BF16)
        per = block // 16
        send1[pl.ds(i * per, per)] = chunk
        return carry

    for n in range(4):
        loads[n].wait()
        lax.fori_loop(n * blocks // 4, (n + 1) * blocks // 4, combine, 0)

    def sector_rows(ref, s):
        return jnp.concatenate(
            [ref[pl.ds(s, cols, stride=8), :], ref[pl.ds(4 + s, cols, stride=8), :]], axis=1
        )

    def neighbour_copies(field):
        return [
            pltpu.make_async_remote_copy(
                nb_send.at[side, field], nb_rcv.at[side, field],
                nb_ssem.at[side, field], nb_rsem.at[side, field],
                device_id={"sector": to}, device_id_type=MESH,
            )
            for side, to in ((0, prv), (1, nxt))
        ]

    def row_k(s):
        mask = cm[pl.ds(s, 1), :]
        return jnp.where(mask == 1, k_stick, jnp.where(mask == 2, k_slip, 0.0))

    def edge_rows(first, last):
        depth = first.shape[1]
        k = row_k(LOCAL - 1)
        return (
            dot(first, ends[0, 0:depth, :]).astype(BF16),
            (dot(last, ends[1, 0:depth, :]) * k).astype(BF16),
        )

    def fill_edges(field, ref):
        k = jnp.broadcast_to(row_k(LOCAL - 1), (16, 128)).astype(BF16)
        values = edge_rows(
            sector_rows(ref, 0).astype(BF16), sector_rows(ref, LOCAL - 1).astype(BF16)
        )
        for side in range(2):
            nb_send[side, field] = jnp.concatenate([values[side], k], axis=0)

    def from_edges(after, before):
        none = jnp.zeros((cols, 128), BF16)
        after = (after.astype(F32) * row_k(LOCAL - 1)).astype(BF16)
        return (
            jnp.concatenate([after, none], axis=1), jnp.concatenate([before, none], axis=1)
        )

    def send_all(src, dst, stage, ssem, rsem):
        def one(i, carry):
            to = peer(i)
            pltpu.make_async_remote_copy(
                src.at[to], dst.at[me], ssem.at[stage], rsem.at[stage],
                device_id={"sector": to}, device_id_type=MESH,
            ).start()
            return carry

        lax.fori_loop(0, ns - 1, one, 0)
        dst[me] = src[me]

    def wait_all(src, dst, stage, ssem, rsem):
        most = pl.ds(0, ns - 1)
        return pltpu.make_async_remote_copy(
            src.at[most], dst.at[most], ssem.at[stage], rsem.at[stage],
            device_id={"sector": nxt}, device_id_type=MESH,
        )

    for copy in smalls:
        copy.wait()
    dof = lax.broadcasted_iota(jnp.int32, (DOF, 128), 0)
    mats_tri = jnp.where(
        jnp.abs(
            lax.broadcasted_iota(jnp.int32, (DOF, DOF), 0)
            - lax.broadcasted_iota(jnp.int32, (DOF, DOF), 1)
        )
        == 1,
        coupling,
        0.0,
    ).astype(BF16)
    eye = jnp.where(
        lax.broadcasted_iota(jnp.int32, (128, 128), 0)
        == lax.broadcasted_iota(jnp.int32, (128, 128), 1),
        1.0,
        0.0,
    ).astype(BF16)
    row8 = lax.broadcasted_iota(jnp.int32, (8, 128), 0)
    total_k = stiff[...]
    for s in range(LOCAL):
        k = row_k(s)
        left = cl[pl.ds(s, 1), :]
        right = cr[pl.ds(s, 1), :]
        at_left = jnp.where(dof == left, 1.0, 0.0).astype(BF16)
        at_right = jnp.where(dof == right, 1.0, 0.0).astype(BF16)
        more = dot(jnp.broadcast_to(k, (8, 128)).astype(BF16), at_left, (1, 1))
        if s > 0:
            mats[s - 1, 0:DOF, :] = dot(at_right, k_left, (1, 1)).astype(BF16)
            mats[s, DOF:2 * DOF, :] = dot(k_left, at_right, (1, 1)).astype(BF16)
            before = jnp.broadcast_to(row_k(s - 1), (8, 128)).astype(BF16)
            more = more + dot(before, at_right, (1, 1))
        else:
            ends[0] = at_right
            mats[0, DOF:DOF + 128, :] = dot(eye, at_right, (1, 1)).astype(BF16)
            mats[0, DOF + 128:2 * DOF, :] = jnp.zeros((128, DOF), BF16)
        if s == LOCAL - 1:
            ends[1] = at_left
            mats[s, 0:128, :] = dot(eye, at_left, (1, 1)).astype(BF16)
            mats[s, 128:DOF, :] = jnp.zeros((128, DOF), BF16)
        mats[s, 2 * DOF:3 * DOF, :] = mats_tri
        total_k = total_k + jnp.where(row8 == s, more[:, 0:128], 0.0)
        total_k = total_k + jnp.where(row8 == LOCAL + s, more[:, 128:256], 0.0)
        k_left = jnp.where(dof == left, jnp.broadcast_to(k, (DOF, 128)), 0.0).astype(BF16)

    fill_edges(0, yp0)
    edge0, edge1, edge2 = [neighbour_copies(field) for field in range(3)]

    pl.semaphore_wait(barrier, ns + 2 * nc - 3)

    for copy in edge0:
        copy.start()
    send_all(send1, rcv1, 0, a_ssem, a_rsem)
    fill_edges(1, yp1)

    def cross(own, next_first, prev_last, dst):
        chain = [prev_last] + own + [next_first]
        for s in range(LOCAL):
            lhs = jnp.concatenate([chain[s + 2], chain[s], chain[s + 1]], axis=1)
            out = dot(lhs, mats[s])
            dst[pl.ds(s, cols, stride=8), :] = out[:, 0:128]
            dst[pl.ds(4 + s, cols, stride=8), :] = out[:, 128:256]

    def edges_in(field):
        return from_edges(nb_rcv[0, field, 0:cols, :], nb_rcv[1, field, 0:cols, :])

    def cross_of(field, ref, dst):
        cross([sector_rows(ref, s).astype(BF16) for s in range(LOCAL)], *edges_in(field), dst)

    def fine_cross_of(field, ref, dst):
        none = jnp.zeros((cols, DOF), BF16)
        after, before = edges_in(field)
        chain = [jnp.concatenate([before, none], axis=0)]
        for s in range(LOCAL):
            value = sector_rows(ref, s)
            high = value.astype(BF16)
            chain.append(jnp.concatenate([high, (value - high.astype(F32)).astype(BF16)], axis=0))
        chain.append(jnp.concatenate([after, none], axis=0))
        for s in range(LOCAL):
            both = dot(jnp.concatenate([chain[s + 2], chain[s], chain[s + 1]], axis=1), mats[s])
            out = both[0:cols] + both[cols:2 * cols]
            dst[pl.ds(s, cols, stride=8), :] = out[:, 0:128]
            dst[pl.ds(4 + s, cols, stride=8), :] = out[:, 128:256]

    def times_k(rows_value):
        tiles = rows_value.reshape(rows_value.shape[0] // 8, 8, 128)
        return (tiles * keff[...][None]).reshape(rows_value.shape)

    for copy in edge0:
        copy.wait()
    more = dot(nb_rcv[1, 0, cols:cols + 16, :], ends[0], (1, 1))[0:8]
    total_k = total_k + jnp.where(row8 == 0, more[:, 0:128], 0.0)
    keff[...] = total_k + jnp.where(row8 == LOCAL, more[:, 128:256], 0.0)
    cross_of(0, yp0, cross0)

    def second(i, carry):
        at = pl.ds(pl.multiple_of(i * block, block), block)
        y0 = yp0[at, :]
        w1 = w_acc[at, :] + cross0[at, :] - times_k(y0)
        v1 = H1 * w1 + e1[at, :]
        p2 = p_acc[at, :] + v1
        y2 = H2 * p2 + e2p[at, :]
        yp2[at, :] = y2
        p_acc[at, :] = p2
        w_acc[at, :] = w1 - damping * v1
        per = block // 16
        send2[pl.ds(i * per, per)] = low_of_pairs(C1 * y0 + C2 * yp1[at, :] + y2).astype(BF16)
        return carry

    lax.fori_loop(0, blocks, second, 0)
    send_all(send2, rcv2, 1, a_ssem, a_rsem)
    fill_edges(2, yp2)
    for copy in edge1 + edge2:
        copy.start()

    smat = pltpu.roll(
        jnp.broadcast_to(slot[...].astype(F32), (sectors, sectors)), 0, 1, stride=1, stride_axis=0
    )
    for k in range(TABLES):
        picks[:, k * sectors:(k + 1) * sectors] = jnp.where(smat == float(k), 1.0, 0.0).astype(BF16)

    coef_load.wait()

    def loads_of(surfaces, acc):
        parts = len(surfaces)
        lhs = jnp.concatenate(surfaces, axis=0).astype(BF16)
        for k in range(0, TABLES, 2):
            u = dot(lhs, coef[k * AERO:(k + 2) * AERO, :], (1, 1)).astype(BF16)
            for n in range(2):
                for c in range(parts):
                    tabled[
                        (k + n) * sectors:(k + n + 1) * sectors, c * AERO:(c + 1) * AERO
                    ] = u[c * sectors:(c + 1) * sectors, n * AERO:(n + 1) * AERO]
        acc[...] = dot(picks[...], tabled[:, 0:parts * AERO])

    def by_sector(received):
        value = received.astype(F32).reshape(ns // 2, 2, 8, received.shape[2])
        first, second_ = swap_halves(value[:, 0], value[:, 1])
        return first.reshape(sectors, -1), second_.reshape(sectors, -1)

    def by_device(first, second_):
        lo, hi = swap_halves(
            first.reshape(ns // 2, 8, 128), second_.reshape(ns // 2, 8, 128)
        )
        return jnp.stack([lo, hi], axis=1).reshape(ns, 8, 128)

    wait_all(send1, rcv1, 0, a_ssem, a_rsem).wait()
    arrived = by_sector(rcv1[...])
    loads_of([arrived[c][:, 0:AERO] for c in range(2)], acc1)
    send3[...] = by_device(acc1[:, 0:AERO], acc1[:, AERO:2 * AERO]).astype(BF16)
    send_all(send3, rcv3, 0, r_ssem, r_rsem)
    loads_of([arrived[c][:, AERO:2 * AERO] for c in range(2)], acc2)
    send5[...] = by_device(acc2[:, 0:AERO], acc2[:, AERO:2 * AERO]).astype(BF16)
    send_all(send5, rcv5, 3, r_ssem, r_rsem)

    for copy in edge1 + edge2:
        copy.wait()
    fine_cross_of(1, yp1, cross1)
    fine_cross_of(2, yp2, cross2)

    def third(i, carry):
        at = pl.ds(pl.multiple_of(i * block, block), block)
        w2 = w_acc[at, :] + cross1[at, :] - times_k(yp1[at, :])
        v2 = H2 * w2 + e2w[at, :]
        p_acc[at, :] = p_acc[at, :] + v2
        w_acc[at, :] = w2 - damping * v2 + cross2[at, :] - times_k(yp2[at, :])
        return carry

    lax.fori_loop(0, blocks, third, 0)

    wait_all(send2, rcv2, 1, a_ssem, a_rsem).wait()
    rest = by_sector(rcv2[...])
    loads_of(
        [rest[c] + HH * acc1[:, c * AERO:(c + 1) * AERO] for c in range(2)], acc2
    )
    send4[...] = by_device(acc2[:, 0:AERO], acc2[:, AERO:2 * AERO]).astype(BF16)
    send_all(send4, rcv4, 1, r_ssem, r_rsem)

    wait_all(send3, rcv3, 0, r_ssem, r_rsem).wait()

    def spread(i, carry):
        per = block // 16
        at = pl.ds(pl.multiple_of(i * block, block), block)
        a0r[at, :] = pairs_of_low(rcv3[pl.ds(i * per, per)].astype(F32))
        return carry

    lax.fori_loop(0, blocks, spread, 0)

    none = jnp.zeros((cols, 128), BF16)
    own = [a0r[pl.ds(s, cols, stride=8), :].astype(BF16) for s in range(LOCAL)]
    nb_low[0], nb_low[1] = edge_rows(own[0], own[LOCAL - 1])
    edge_low = [
        pltpu.make_async_remote_copy(
            nb_low.at[side], nb_low_rcv.at[side], low_ssem.at[side], low_rsem.at[side],
            device_id={"sector": to}, device_id_type=MESH,
        )
        for side, to in ((0, prv), (1, nxt))
    ]
    for copy in edge_low:
        copy.start()

    wait_all(send5, rcv5, 3, r_ssem, r_rsem).wait()

    def close_p(i, carry):
        per = block // 16
        at = pl.ds(pl.multiple_of(i * block, block), block)
        p3 = p_acc[at, :] + pairs_of_low(rcv5[pl.ds(i * per, per)].astype(F32))
        st[0, at, :] = p3
        return carry + jnp.sum((p3 * p3).reshape(block // 8, 8, 128), axis=0)

    squares = lax.fori_loop(0, blocks, close_p, jnp.zeros((8, 128), F32))

    for copy in edge_low:
        copy.wait()
    cross(
        [jnp.concatenate([v, none], axis=1) for v in own],
        *from_edges(nb_low_rcv[0], nb_low_rcv[1]),
        cross0,
    )

    def fourth(i, carry):
        at = pl.ds(pl.multiple_of(i * block, block), block)
        w_acc[at, :] = w_acc[at, :] + HH * (cross0[at, :] - times_k(a0r[at, :]))
        return carry

    lax.fori_loop(0, blocks, fourth, 0)

    wait_all(send4, rcv4, 1, r_ssem, r_rsem).wait()

    def fifth(i, carry):
        per = block // 16
        at = pl.ds(pl.multiple_of(i * block, block), block)
        w3 = w_acc[at, :] + pairs_of_low(rcv4[pl.ds(i * per, per)].astype(F32))
        st[1, at, :] = w3
        return carry + jnp.sum((w3 * w3).reshape(block // 8, 8, 128), axis=0)

    squares = lax.fori_loop(0, blocks, fifth, squares)

    part[...] = jnp.sum(squares, axis=0, keepdims=True)

    low = lax.rem(me, half)
    spot = high * nc + mycol

    def over_high(i, carry):
        to_high, to = high_peer(i)
        pltpu.make_async_remote_copy(
            part, colsum.at[spot], a_ssem.at[2], a_rsem.at[2],
            device_id={"sector": low + half * to_high, "col": to},
            device_id_type=MESH,
        ).start()
        return carry

    lax.fori_loop(0, 2 * nc - 1, over_high, 0)
    colsum[spot] = part[...]
    most = pl.ds(0, 2 * nc - 1)
    pltpu.make_async_remote_copy(
        colsum.at[most], colsum.at[most], a_ssem.at[2], a_rsem.at[2],
        device_id={"sector": nxt}, device_id_type=MESH,
    ).wait()
    secpart[...] = jnp.sum(colsum[...], axis=0)

    def over_low(i, carry):
        to = low_peer(i)
        pltpu.make_async_remote_copy(
            secpart, secsum.at[low], r_ssem.at[2], r_rsem.at[2],
            device_id={"sector": high * half + to}, device_id_type=MESH,
        ).start()
        return carry

    lax.fori_loop(0, half - 1, over_low, 0)
    secsum[low] = secpart[...]
    most_low = pl.ds(0, half - 1)
    pltpu.make_async_remote_copy(
        secsum.at[most_low], secsum.at[most_low], r_ssem.at[2], r_rsem.at[2],
        device_id={"sector": nxt}, device_id_type=MESH,
    ).wait()
    everything = jnp.sum(jnp.sum(secsum[...], axis=0), axis=1, keepdims=True)
    growth_ref[...] = jnp.broadcast_to(jnp.sqrt(everything / total_count + 1e-6), (1, 128))


def per_device(
    ns, nc, prev_nodes, stiffness, aero_coef, offset_slot, contact_left, contact_right, contact_mask
):
    cols = prev_nodes.shape[2]
    rows = cols * 8
    sectors = ns * LOCAL
    x = prev_nodes.reshape(8, cols, LOCAL, 2, 128).transpose(0, 1, 3, 2, 4).reshape(8, rows, 128)
    stiff = stiffness.reshape(LOCAL, 2, 128).transpose(1, 0, 2).reshape(8, 128)
    vm = pltpu.VMEM
    big = vm((rows, 128), F32)
    ints = vm((LOCAL, 128), jnp.int32)
    dma = pltpu.SemaphoreType.DMA
    any_spec = pl.BlockSpec(memory_space=pl.ANY)
    state, growth = pl.pallas_call(
        functools.partial(kernel, ns, nc, float(2 * cols * nc * sectors * DOF)),
        out_shape=(
            pltpu.VMEM((2, rows, 128), F32),
            pltpu.VMEM((1, 128), F32),
        ),
        in_specs=[any_spec] * 7,
        out_specs=(pl.BlockSpec(memory_space=pltpu.VMEM), pl.BlockSpec(memory_space=pltpu.VMEM)),
        scratch_shapes=[
            vm((8, rows, 128), F32),
            vm((8, 128), F32),
            vm((TABLES * AERO, AERO), BF16),
            vm((1, sectors), jnp.int32),
            ints, ints, ints,
            vm((8, 128), F32),
            vm((LOCAL, 3 * DOF, DOF), BF16),
            vm((2, DOF, 128), BF16),
            vm((sectors, TABLES * sectors), BF16),
            vm((TABLES * sectors, 2 * AERO), BF16),
            big, big, big, big, big, big, big,
            big, big, big, big, big,
            vm((ns, 8, 256), BF16), vm((ns, 8, 256), BF16),
            vm((ns, 8, 128), BF16), vm((ns, 8, 128), BF16),
            vm((ns, 8, 128), BF16), vm((ns, 8, 128), BF16),
            vm((ns, 8, 128), BF16), vm((ns, 8, 128), BF16),
            vm((ns, 8, 128), BF16), vm((ns, 8, 128), BF16),
            vm((2, 3, cols + 16, 128), BF16), vm((2, 3, cols + 16, 128), BF16),
            vm((2, cols, 128), BF16), vm((2, cols, 128), BF16),
            vm((sectors, 2 * AERO), F32),
            vm((sectors, 2 * AERO), F32),
            vm((1, 128), F32),
            vm((2 * nc, 1, 128), F32),
            vm((ns // 2, 1, 128), F32),
            vm((1, 128), F32),
            dma((5,)), dma((5,)),
            dma((2, 3)), dma((2, 3)),
            dma((3,)), dma((3,)), dma((4,)), dma((4,)),
            dma((2,)), dma((2,)),
        ],
        compiler_params=pltpu.CompilerParams(
            collective_id=0, has_side_effects=True, vmem_limit_bytes=60 << 20
        ),
        name="sweep",
    )(
        x, stiff, aero_coef.reshape(TABLES * AERO, AERO), offset_slot.reshape(1, sectors),
        contact_left, contact_right, contact_mask,
    )
    value = growth[0, 0]
    scaled = state / value
    scaled = scaled.reshape(2, cols, 2, LOCAL, 128).transpose(0, 1, 3, 2, 4)
    return scaled.reshape(2, cols, LOCAL, DOF), value


def solution(mesh):
    ns, nc = mesh.shape["sector"], mesh.shape["col"]
    placed = (
        P(None, None, "col", "sector", None),
        P("sector", None),
        P(),
        P(),
        P("sector", None),
        P("sector", None),
        P("sector", None),
    )
    return jax.shard_map(
        functools.partial(per_device, ns, nc),
        mesh=mesh,
        in_specs=placed,
        out_specs=(P(None, "col", "sector", None), P()),
        check_vma=False,
    )
```

```python
import functools
import math

import jax
import jax.numpy as jnp
from jax import lax
from jax.experimental import pallas as pl
from jax.experimental.pallas import tpu as pltpu
from jax.sharding import PartitionSpec as P

DOF = 256
AERO = 128
TABLES = 32
LOCAL = 4
MESH = pl.DeviceIdType.MESH
F32 = jnp.float32
BF16 = jnp.bfloat16

time_step = 0.25
coupling = 0.5
damping = 0.1
k_stick = 4.0
k_slip = 1.0


def quad_tables():
    root = 1.0 / math.sqrt(5.0)
    tau = [0.0, (1.0 - root) / 2.0, (1.0 + root) / 2.0, 1.0]
    table = []
    for m in range(3):
        table_row = []
        for j in range(4):
            coeffs = [1.0]
            scale = 1.0
            for k in range(4):
                if k != j:
                    widened = [0.0] * (len(coeffs) + 1)
                    for power in range(len(coeffs)):
                        widened[power + 1] = widened[power + 1] + coeffs[power]
                        widened[power] = widened[power] - tau[k] * coeffs[power]
                    coeffs = widened
                    scale = scale * (tau[j] - tau[k])
            integral = 0.0
            for power in range(len(coeffs)):
                integral = integral + coeffs[power] * (
                    tau[m + 1] ** (power + 1) - tau[m] ** (power + 1)
                ) / (power + 1)
            table_row.append(integral / scale * time_step)
        table.append(table_row)
    steps = [(tau[m + 1] - tau[m]) * time_step for m in range(3)]
    return (table, steps)


S, H = quad_tables()
H1, H2 = H[1], H[2]
C1 = (1.0 - damping * H1) * (1.0 - damping * H2)
C2 = 1.0 - damping * H2
C3 = H1 + H2 * (1.0 - damping * H1)
HH = H1 * H2


def swap_halves(a, b):
    axis = a.ndim - 2
    low = lax.broadcasted_iota(jnp.int32, a.shape, axis) < 4
    return (
        jnp.where(low, a, pltpu.roll(b, 4, axis)),
        jnp.where(low, pltpu.roll(a, 4, axis), b),
    )


def low_of_pairs(rows):
    tiles = rows.reshape(rows.shape[0] // 16, 2, 8, 128)
    return swap_halves(tiles[:, 0], tiles[:, 1])[0]


def pairs_of_low(chunks):
    low = lax.broadcasted_iota(jnp.int32, chunks.shape, 1) < 4
    first = jnp.where(low, chunks, 0.0)
    second = jnp.where(low, pltpu.roll(chunks, 4, 1), 0.0)
    return jnp.stack([first, second], axis=1).reshape(chunks.shape[0] * 16, 128)


def far_first(step, length):
    return lax.rem(length // 2 + length + (1 - 2 * lax.rem(step, 2)) * ((step + 1) // 2), length)


def dot(a, b, dims=(1, 0)):
    return lax.dot_general(
        a, b, (((dims[0],), (dims[1],)), ((), ())), preferred_element_type=F32
    )


def kernel(
    ns, nc, total_count,
    x_hbm, stiff_hbm, coef_hbm, slot_hbm, cl_hbm, cr_hbm, cm_hbm,
    st, growth_ref,
    xs, stiff, coef, slot, cl, cr, cm,
    keff, extra_k, mats, ends, picks, tabled,
    yp0, yp1, yp2, a0r, cross0, cross1, cross2,
    w_acc, p_acc, e1, e2p, e2w,
    send1, rcv1, send2, rcv2, send3, rcv3, send4, rcv4,
    nb_send, nb_rcv, nb_low, nb_low_rcv, acc1, acc2, part, colsum, secsum, secpart,
    load_sem, small_sem,
    nb_ssem, nb_rsem, a_ssem, a_rsem, r_ssem, r_rsem,
    low_ssem, low_rsem,
):
    me = lax.axis_index("sector")
    mycol = lax.axis_index("col")
    rows = xs.shape[1]
    cols = 2 * ns
    sectors = LOCAL * ns
    block = min(64, rows // 4)
    blocks = rows // block
    nxt = lax.rem(me + 1, ns)
    prv = lax.rem(me + ns - 1, ns)

    barrier = pltpu.get_barrier_semaphore()

    rings = ns // 4
    half = ns // 2
    wide = nc // 2
    core, along, high = lax.rem(me, 2), lax.rem(me // 2, rings), me // half
    across, lane = mycol // 2, lax.rem(mycol, 2)

    def peer(i):
        step, rest = far_first(i // 4, rings), lax.rem(i, 4)
        return (
            lax.rem(high + 1 - rest // 2, 2) * half
            + lax.rem(along + step, rings) * 2
            + lax.rem(core + 1 - lax.rem(rest, 2), 2)
        )

    def low_peer(i):
        step = far_first(i // 2, rings)
        return lax.rem(along + step, rings) * 2 + lax.rem(core + 1 - lax.rem(i, 2), 2)

    def high_peer(i):
        step, rest = far_first(i // 4, wide), lax.rem(i, 4)
        to = lax.rem(across + step, wide) * 2 + lax.rem(lane + 1 - lax.rem(rest, 2), 2)
        return lax.rem(high + 1 - rest // 2, 2), to

    def greet_sector(i, carry):
        pl.semaphore_signal(
            barrier, inc=1, device_id={"sector": peer(i)}, device_id_type=MESH
        )
        return carry

    def greet_other(i, carry):
        pl.semaphore_signal(
            barrier, inc=1,
            device_id={"sector": lax.rem(me + ns // 2, ns), "col": lax.rem(mycol + i, nc)},
            device_id_type=MESH,
        )
        return carry

    def greet_col(i, carry):
        pl.semaphore_signal(
            barrier, inc=1, device_id={"col": lax.rem(mycol + i, nc)}, device_id_type=MESH
        )
        return carry

    smalls = [
        pltpu.make_async_copy(src, dst, small_sem.at[n])
        for n, (src, dst) in enumerate(
            [(cl_hbm, cl), (cm_hbm, cm), (cr_hbm, cr), (stiff_hbm, stiff), (slot_hbm, slot)]
        )
    ]
    for copy in smalls:
        copy.start()
    quarter = rows // 4
    loads = [
        pltpu.make_async_copy(
            x_hbm.at[:, pl.ds(n * quarter, quarter), :],
            xs.at[:, pl.ds(n * quarter, quarter), :],
            load_sem.at[n],
        )
        for n in range(4)
    ]
    for copy in loads:
        copy.start()
    lax.fori_loop(0, ns - 1, greet_sector, 0)
    lax.fori_loop(1, nc, greet_other, 0)
    lax.fori_loop(1, nc, greet_col, 0)
    coef_load = pltpu.make_async_copy(coef_hbm, coef, load_sem.at[4])
    coef_load.start()

    def row_k(s):
        mask = cm[pl.ds(s, 1), :]
        return jnp.where(mask == 1, k_stick, jnp.where(mask == 2, k_slip, 0.0))

    for copy in smalls[0:4]:
        copy.wait()
    dof = lax.broadcasted_iota(jnp.int32, (DOF, 128), 0)
    mats_tri = jnp.where(
        jnp.abs(
            lax.broadcasted_iota(jnp.int32, (DOF, DOF), 0)
            - lax.broadcasted_iota(jnp.int32, (DOF, DOF), 1)
        )
        == 1,
        coupling,
        0.0,
    ).astype(BF16)
    eye = jnp.where(
        lax.broadcasted_iota(jnp.int32, (128, 128), 0)
        == lax.broadcasted_iota(jnp.int32, (128, 128), 1),
        1.0,
        0.0,
    ).astype(BF16)
    row8 = lax.broadcasted_iota(jnp.int32, (8, 128), 0)
    total_k = stiff[...]
    for s in range(LOCAL):
        k = row_k(s)
        left = cl[pl.ds(s, 1), :]
        right = cr[pl.ds(s, 1), :]
        at_left = jnp.where(dof == left, 1.0, 0.0).astype(BF16)
        at_right = jnp.where(dof == right, 1.0, 0.0).astype(BF16)
        more = dot(jnp.broadcast_to(k, (8, 128)).astype(BF16), at_left, (1, 1))
        if s > 0:
            mats[s - 1, 0:DOF, :] = dot(at_right, k_left, (1, 1)).astype(BF16)
            mats[s, DOF:2 * DOF, :] = dot(k_left, at_right, (1, 1)).astype(BF16)
            before = jnp.broadcast_to(row_k(s - 1), (8, 128)).astype(BF16)
            more = more + dot(before, at_right, (1, 1))
        else:
            ends[0] = at_right
            mats[0, DOF:DOF + 128, :] = dot(eye, at_right, (1, 1)).astype(BF16)
            mats[0, DOF + 128:2 * DOF, :] = jnp.zeros((128, DOF), BF16)
        if s == LOCAL - 1:
            ends[1] = at_left
            mats[s, 0:128, :] = dot(eye, at_left, (1, 1)).astype(BF16)
            mats[s, 128:DOF, :] = jnp.zeros((128, DOF), BF16)
        mats[s, 2 * DOF:3 * DOF, :] = mats_tri
        total_k = total_k + jnp.where(row8 == s, more[:, 0:128], 0.0)
        total_k = total_k + jnp.where(row8 == LOCAL + s, more[:, 128:256], 0.0)
        k_left = jnp.where(dof == left, jnp.broadcast_to(k, (DOF, 128)), 0.0).astype(BF16)
    keff[...] = total_k

    def combine(i, carry):
        at = pl.ds(pl.multiple_of(i * block, block), block)
        p = [xs[2 * j, at, :] for j in range(4)]
        w = [xs[2 * j + 1, at, :] for j in range(4)]

        def quad(m, v):
            out = v[0] * float(S[m][0])
            for j in range(1, 4):
                out = out + float(S[m][j]) * v[j]
            return out

        y0 = quad(0, p)
        v0 = quad(0, w)
        p1 = p[0] + v0
        y1 = quad(1, p) + H1 * (p1 - p[1])
        yp0[at, :] = y0
        yp1[at, :] = y1
        p_acc[at, :] = p1
        w_acc[at, :] = w[0] - damping * v0
        e1[at, :] = quad(1, w) - H1 * w[1]
        e2p[at, :] = quad(2, p) - H2 * p[2]
        e2w[at, :] = quad(2, w) - H2 * w[2]
        per = block // 16
        send1[pl.ds(i * per, per), :, 0:128] = low_of_pairs(y0).astype(BF16)
        send1[pl.ds(i * per, per), :, 128:256] = low_of_pairs(C3 * y0 + H2 * y1).astype(BF16)
        return carry

    for n in range(4):
        loads[n].wait()
        lax.fori_loop(n * blocks // 4, (n + 1) * blocks // 4, combine, 0)

    def sector_rows(ref, s):
        return jnp.concatenate(
            [ref[pl.ds(s, cols, stride=8), :], ref[pl.ds(4 + s, cols, stride=8), :]], axis=1
        )

    def neighbour_copies(field):
        return [
            pltpu.make_async_remote_copy(
                nb_send.at[side, field], nb_rcv.at[side, field],
                nb_ssem.at[side, field], nb_rsem.at[side, field],
                device_id={"sector": to}, device_id_type=MESH,
            )
            for side, to in ((0, prv), (1, nxt))
        ]

    def edge_rows(first, last):
        depth = first.shape[1]
        k = row_k(LOCAL - 1)
        return (
            dot(first, ends[0, 0:depth, :]).astype(BF16),
            (dot(last, ends[1, 0:depth, :]) * k).astype(BF16),
        )

    def fill_edges(field, ref):
        k = jnp.broadcast_to(row_k(LOCAL - 1), (16, 128)).astype(BF16)
        values = edge_rows(
            sector_rows(ref, 0).astype(BF16), sector_rows(ref, LOCAL - 1).astype(BF16)
        )
        for side in range(2):
            nb_send[side, field] = jnp.concatenate([values[side], k], axis=0)

    def from_edges(after, before):
        none = jnp.zeros((cols, 128), BF16)
        after = (after.astype(F32) * row_k(LOCAL - 1)).astype(BF16)
        return (
            jnp.concatenate([after, none], axis=1), jnp.concatenate([before, none], axis=1)
        )

    def send_all(src, dst, stage, ssem, rsem):
        def one(i, carry):
            to = peer(i)
            pltpu.make_async_remote_copy(
                src.at[to], dst.at[me], ssem.at[stage], rsem.at[stage],
                device_id={"sector": to}, device_id_type=MESH,
            ).start()
            return carry

        lax.fori_loop(0, ns - 1, one, 0)
        dst[me] = src[me]

    def wait_all(src, dst, stage, ssem, rsem):
        most = pl.ds(0, ns - 1)
        return pltpu.make_async_remote_copy(
            src.at[most], dst.at[most], ssem.at[stage], rsem.at[stage],
            device_id={"sector": nxt}, device_id_type=MESH,
        )

    fill_edges(0, yp0)
    edge0, edge1, edge2 = [neighbour_copies(field) for field in range(3)]

    pl.semaphore_wait(barrier, ns + 2 * nc - 3)

    for copy in edge0:
        copy.start()
    send_all(send1, rcv1, 0, a_ssem, a_rsem)
    fill_edges(1, yp1)

    def cross(own, next_first, prev_last, dst):
        chain = [prev_last] + own + [next_first]
        for s in range(LOCAL):
            lhs = jnp.concatenate([chain[s + 2], chain[s], chain[s + 1]], axis=1)
            out = dot(lhs, mats[s])
            dst[pl.ds(s, cols, stride=8), :] = out[:, 0:128]
            dst[pl.ds(4 + s, cols, stride=8), :] = out[:, 128:256]

    def edges_in(field):
        return from_edges(nb_rcv[0, field, 0:cols, :], nb_rcv[1, field, 0:cols, :])

    def fine_cross_of(field, ref, dst):
        none = jnp.zeros((cols, DOF), BF16)
        after, before = edges_in(field)
        chain = [jnp.concatenate([before, none], axis=0)]
        for s in range(LOCAL):
            value = sector_rows(ref, s)
            high = value.astype(BF16)
            chain.append(jnp.concatenate([high, (value - high.astype(F32)).astype(BF16)], axis=0))
        chain.append(jnp.concatenate([after, none], axis=0))
        for s in range(LOCAL):
            both = dot(jnp.concatenate([chain[s + 2], chain[s], chain[s + 1]], axis=1), mats[s])
            out = both[0:cols] + both[cols:2 * cols]
            dst[pl.ds(s, cols, stride=8), :] = out[:, 0:128]
            dst[pl.ds(4 + s, cols, stride=8), :] = out[:, 128:256]

    def times_k(rows_value):
        tiles = rows_value.reshape(rows_value.shape[0] // 8, 8, 128)
        return (tiles * keff[...][None]).reshape(rows_value.shape)

    none = jnp.zeros((cols, DOF), BF16)
    cross([sector_rows(yp0, s).astype(BF16) for s in range(LOCAL)], none, none, cross0)

    def second(i, carry):
        at = pl.ds(pl.multiple_of(i * block, block), block)
        y0 = yp0[at, :]
        w1 = w_acc[at, :] + cross0[at, :] - times_k(y0)
        v1 = H1 * w1 + e1[at, :]
        p2 = p_acc[at, :] + v1
        y2 = H2 * p2 + e2p[at, :]
        yp2[at, :] = y2
        p_acc[at, :] = p2
        w_acc[at, :] = w1 - damping * v1
        cross1[at, :] = C1 * y0 + C2 * yp1[at, :] + y2
        return carry

    lax.fori_loop(0, blocks, second, 0)

    for copy in edge0:
        copy.wait()
    after, before = edges_in(0)
    out = dot(before[:, 0:128], mats[0, DOF:DOF + 128, :])
    cross0[pl.ds(0, cols, stride=8), :] = out[:, 0:128]
    cross0[pl.ds(4, cols, stride=8), :] = out[:, 128:256]
    out = dot(after[:, 0:128], mats[LOCAL - 1, 0:128, :])
    cross0[pl.ds(LOCAL - 1, cols, stride=8), :] = out[:, 0:128]
    cross0[pl.ds(4 + LOCAL - 1, cols, stride=8), :] = out[:, 128:256]
    more = dot(nb_rcv[1, 0, cols:cols + 16, :], ends[0], (1, 1))[0:8]
    extra_k[...] = jnp.where(row8 == 0, more[:, 0:128], 0.0) + jnp.where(
        row8 == LOCAL, more[:, 128:256], 0.0
    )
    place = lax.broadcasted_iota(jnp.int32, (block // 8, 8, 128), 1) % LOCAL
    outer = (place == 0) | (place == LOCAL - 1)

    def correction(at):
        shape = (block // 8, 8, 128)
        value = jnp.where(outer, cross0[at, :].reshape(shape), 0.0)
        return (value - extra_k[...][None] * yp0[at, :].reshape(shape)).reshape(block, 128)

    def correct_v(i, carry):
        at = pl.ds(pl.multiple_of(i * block, block), block)
        per = block // 16
        send2[pl.ds(i * per, per)] = low_of_pairs(cross1[at, :] + HH * correction(at)).astype(BF16)
        return carry

    lax.fori_loop(0, blocks, correct_v, 0)
    send_all(send2, rcv2, 1, a_ssem, a_rsem)

    def correct_rest(i, carry):
        at = pl.ds(pl.multiple_of(i * block, block), block)
        change = correction(at)
        yp2[at, :] = yp2[at, :] + HH * change
        p_acc[at, :] = p_acc[at, :] + H1 * change
        w_acc[at, :] = w_acc[at, :] + (1.0 - damping * H1) * change
        return carry

    lax.fori_loop(0, blocks, correct_rest, 0)
    keff[...] = keff[...] + extra_k[...]
    fill_edges(2, yp2)
    for copy in edge1 + edge2:
        copy.start()

    smalls[4].wait()
    smat = pltpu.roll(
        jnp.broadcast_to(slot[...].astype(F32), (sectors, sectors)), 0, 1, stride=1, stride_axis=0
    )
    for k in range(TABLES):
        picks[:, k * sectors:(k + 1) * sectors] = jnp.where(smat == float(k), 1.0, 0.0).astype(BF16)

    coef_load.wait()

    def loads_of(surfaces, acc):
        parts = len(surfaces)
        lhs = jnp.concatenate(list(surfaces), axis=0).astype(BF16)
        for k in range(0, TABLES, 2):
            u = dot(lhs, coef[k * AERO:(k + 2) * AERO, :], (1, 1)).astype(BF16)
            for n in range(2):
                for c in range(parts):
                    tabled[
                        (k + n) * sectors:(k + n + 1) * sectors, c * AERO:(c + 1) * AERO
                    ] = u[c * sectors:(c + 1) * sectors, n * AERO:(n + 1) * AERO]
        acc[...] = dot(picks[...], tabled[:, 0:parts * AERO])

    def by_sector(received):
        value = received.astype(F32).reshape(ns // 2, 2, 8, received.shape[2])
        first, second_ = swap_halves(value[:, 0], value[:, 1])
        return first.reshape(sectors, -1), second_.reshape(sectors, -1)

    def by_device(first, second_):
        lo, hi = swap_halves(
            first.reshape(ns // 2, 8, 128), second_.reshape(ns // 2, 8, 128)
        )
        return jnp.stack([lo, hi], axis=1).reshape(ns, 8, 128)

    wait_all(send1, rcv1, 0, a_ssem, a_rsem).wait()
    arrived = by_sector(rcv1[...])
    loads_of([arrived[c][:, f * AERO:(f + 1) * AERO] for f in range(2) for c in range(2)], acc2)
    for n in range(2):
        at = 2 * n * AERO
        send3[:, :, n * AERO:(n + 1) * AERO] = by_device(
            acc2[:, at:at + AERO], acc2[:, at + AERO:at + 2 * AERO]
        ).astype(BF16)
    send_all(send3, rcv3, 0, r_ssem, r_rsem)

    wait_all(send2, rcv2, 1, a_ssem, a_rsem).wait()
    rest = by_sector(rcv2[...])
    loads_of([rest[c] + HH * acc2[:, c * AERO:(c + 1) * AERO] for c in range(2)], acc1)
    send4[...] = by_device(acc1[:, 0:AERO], acc1[:, AERO:2 * AERO]).astype(BF16)
    send_all(send4, rcv4, 1, r_ssem, r_rsem)

    for copy in edge1 + edge2:
        copy.wait()
    fine_cross_of(1, yp1, cross1)
    fine_cross_of(2, yp2, cross2)

    def third(i, carry):
        at = pl.ds(pl.multiple_of(i * block, block), block)
        w2 = w_acc[at, :] + cross1[at, :] - times_k(yp1[at, :])
        v2 = H2 * w2 + e2w[at, :]
        p_acc[at, :] = p_acc[at, :] + v2
        w_acc[at, :] = w2 - damping * v2 + cross2[at, :] - times_k(yp2[at, :])
        return carry

    lax.fori_loop(0, blocks, third, 0)

    wait_all(send3, rcv3, 0, r_ssem, r_rsem).wait()

    def spread(i, carry):
        per = block // 16
        at = pl.ds(pl.multiple_of(i * block, block), block)
        got = rcv3[pl.ds(i * per, per)].astype(F32)
        a0r[at, :] = pairs_of_low(got[:, :, 0:128])
        p3 = p_acc[at, :] + pairs_of_low(got[:, :, 128:256])
        st[0, at, :] = p3
        return carry + jnp.sum((p3 * p3).reshape(block // 8, 8, 128), axis=0)

    squares = lax.fori_loop(0, blocks, spread, jnp.zeros((8, 128), F32))

    none = jnp.zeros((cols, 128), BF16)
    own = [a0r[pl.ds(s, cols, stride=8), :].astype(BF16) for s in range(LOCAL)]
    nb_low[0], nb_low[1] = edge_rows(own[0], own[LOCAL - 1])
    edge_low = [
        pltpu.make_async_remote_copy(
            nb_low.at[side], nb_low_rcv.at[side], low_ssem.at[side], low_rsem.at[side],
            device_id={"sector": to}, device_id_type=MESH,
        )
        for side, to in ((0, prv), (1, nxt))
    ]
    for copy in edge_low:
        copy.start()

    for copy in edge_low:
        copy.wait()
    cross(
        [jnp.concatenate([v, none], axis=1) for v in own],
        *from_edges(nb_low_rcv[0], nb_low_rcv[1]),
        cross0,
    )

    def fourth(i, carry):
        at = pl.ds(pl.multiple_of(i * block, block), block)
        w_acc[at, :] = w_acc[at, :] + HH * (cross0[at, :] - times_k(a0r[at, :]))
        return carry

    lax.fori_loop(0, blocks, fourth, 0)

    wait_all(send4, rcv4, 1, r_ssem, r_rsem).wait()

    def close(i, carry):
        per = block // 16
        at = pl.ds(pl.multiple_of(i * block, block), block)
        w3 = w_acc[at, :] + pairs_of_low(rcv4[pl.ds(i * per, per)].astype(F32))
        st[1, at, :] = w3
        return carry + jnp.sum((w3 * w3).reshape(block // 8, 8, 128), axis=0)

    squares = lax.fori_loop(0, blocks, close, squares)

    part[...] = jnp.sum(squares, axis=0, keepdims=True)

    low = lax.rem(me, half)
    spot = high * nc + mycol

    def over_high(i, carry):
        to_high, to = high_peer(i)
        pltpu.make_async_remote_copy(
            part, colsum.at[spot], a_ssem.at[2], a_rsem.at[2],
            device_id={"sector": low + half * to_high, "col": to},
            device_id_type=MESH,
        ).start()
        return carry

    lax.fori_loop(0, 2 * nc - 1, over_high, 0)
    colsum[spot] = part[...]
    most = pl.ds(0, 2 * nc - 1)
    pltpu.make_async_remote_copy(
        colsum.at[most], colsum.at[most], a_ssem.at[2], a_rsem.at[2],
        device_id={"sector": nxt}, device_id_type=MESH,
    ).wait()
    secpart[...] = jnp.sum(colsum[...], axis=0)

    def over_low(i, carry):
        to = low_peer(i)
        pltpu.make_async_remote_copy(
            secpart, secsum.at[low], r_ssem.at[2], r_rsem.at[2],
            device_id={"sector": high * half + to}, device_id_type=MESH,
        ).start()
        return carry

    lax.fori_loop(0, half - 1, over_low, 0)
    secsum[low] = secpart[...]
    most_low = pl.ds(0, half - 1)
    pltpu.make_async_remote_copy(
        secsum.at[most_low], secsum.at[most_low], r_ssem.at[2], r_rsem.at[2],
        device_id={"sector": nxt}, device_id_type=MESH,
    ).wait()
    everything = jnp.sum(jnp.sum(secsum[...], axis=0), axis=1, keepdims=True)
    growth_ref[...] = jnp.broadcast_to(jnp.sqrt(everything / total_count + 1e-6), (1, 128))


def per_device(
    ns, nc, prev_nodes, stiffness, aero_coef, offset_slot, contact_left, contact_right, contact_mask
):
    cols = prev_nodes.shape[2]
    rows = cols * 8
    sectors = ns * LOCAL
    x = prev_nodes.reshape(8, cols, LOCAL, 2, 128).transpose(0, 1, 3, 2, 4).reshape(8, rows, 128)
    stiff = stiffness.reshape(LOCAL, 2, 128).transpose(1, 0, 2).reshape(8, 128)
    vm = pltpu.VMEM
    big = vm((rows, 128), F32)
    ints = vm((LOCAL, 128), jnp.int32)
    dma = pltpu.SemaphoreType.DMA
    any_spec = pl.BlockSpec(memory_space=pl.ANY)
    state, growth = pl.pallas_call(
        functools.partial(kernel, ns, nc, float(2 * cols * nc * sectors * DOF)),
        out_shape=(
            pltpu.VMEM((2, rows, 128), F32),
            pltpu.VMEM((1, 128), F32),
        ),
        in_specs=[any_spec] * 7,
        out_specs=(pl.BlockSpec(memory_space=pltpu.VMEM), pl.BlockSpec(memory_space=pltpu.VMEM)),
        scratch_shapes=[
            vm((8, rows, 128), F32),
            vm((8, 128), F32),
            vm((TABLES * AERO, AERO), BF16),
            vm((1, sectors), jnp.int32),
            ints, ints, ints,
            vm((8, 128), F32),
            vm((8, 128), F32),
            vm((LOCAL, 3 * DOF, DOF), BF16),
            vm((2, DOF, 128), BF16),
            vm((sectors, TABLES * sectors), BF16),
            vm((TABLES * sectors, 4 * AERO), BF16),
            big, big, big, big, big, big, big,
            big, big, big, big, big,
            vm((ns, 8, 256), BF16), vm((ns, 8, 256), BF16),
            vm((ns, 8, 128), BF16), vm((ns, 8, 128), BF16),
            vm((ns, 8, 256), BF16), vm((ns, 8, 256), BF16),
            vm((ns, 8, 128), BF16), vm((ns, 8, 128), BF16),
            vm((2, 3, cols + 16, 128), BF16), vm((2, 3, cols + 16, 128), BF16),
            vm((2, cols, 128), BF16), vm((2, cols, 128), BF16),
            vm((sectors, 2 * AERO), F32),
            vm((sectors, 4 * AERO), F32),
            vm((1, 128), F32),
            vm((2 * nc, 1, 128), F32),
            vm((ns // 2, 1, 128), F32),
            vm((1, 128), F32),
            dma((5,)), dma((5,)),
            dma((2, 3)), dma((2, 3)),
            dma((3,)), dma((3,)), dma((3,)), dma((3,)),
            dma((2,)), dma((2,)),
        ],
        compiler_params=pltpu.CompilerParams(
            collective_id=0, has_side_effects=True, vmem_limit_bytes=60 << 20
        ),
        name="sweep",
    )(
        x, stiff, aero_coef.reshape(TABLES * AERO, AERO), offset_slot.reshape(1, sectors),
        contact_left, contact_right, contact_mask,
    )
    value = growth[0, 0]
    scaled = state / value
    scaled = scaled.reshape(2, cols, 2, LOCAL, 128).transpose(0, 1, 3, 2, 4)
    return scaled.reshape(2, cols, LOCAL, DOF), value


def solution(mesh):
    ns, nc = mesh.shape["sector"], mesh.shape["col"]
    placed = (
        P(None, None, "col", "sector", None),
        P("sector", None),
        P(),
        P(),
        P("sector", None),
        P("sector", None),
        P("sector", None),
    )
    return jax.shard_map(
        functools.partial(per_device, ns, nc),
        mesh=mesh,
        in_specs=placed,
        out_specs=(P(None, "col", "sector", None), P()),
        check_vma=False,
    )
```

```python
import functools
import math

import jax
import jax.numpy as jnp
from jax import lax
from jax.experimental import pallas as pl
from jax.experimental.pallas import tpu as pltpu
from jax.sharding import PartitionSpec as P

DOF = 256
AERO = 128
TABLES = 32
LOCAL = 4
MESH = pl.DeviceIdType.MESH
F32 = jnp.float32
BF16 = jnp.bfloat16

time_step = 0.25
coupling = 0.5
damping = 0.1
k_stick = 4.0
k_slip = 1.0


def quad_tables():
    root = 1.0 / math.sqrt(5.0)
    tau = [0.0, (1.0 - root) / 2.0, (1.0 + root) / 2.0, 1.0]
    table = []
    for m in range(3):
        table_row = []
        for j in range(4):
            coeffs = [1.0]
            scale = 1.0
            for k in range(4):
                if k != j:
                    widened = [0.0] * (len(coeffs) + 1)
                    for power in range(len(coeffs)):
                        widened[power + 1] = widened[power + 1] + coeffs[power]
                        widened[power] = widened[power] - tau[k] * coeffs[power]
                    coeffs = widened
                    scale = scale * (tau[j] - tau[k])
            integral = 0.0
            for power in range(len(coeffs)):
                integral = integral + coeffs[power] * (
                    tau[m + 1] ** (power + 1) - tau[m] ** (power + 1)
                ) / (power + 1)
            table_row.append(integral / scale * time_step)
        table.append(table_row)
    steps = [(tau[m + 1] - tau[m]) * time_step for m in range(3)]
    return (table, steps)


S, H = quad_tables()
H1, H2 = H[1], H[2]
C1 = (1.0 - damping * H1) * (1.0 - damping * H2)
C2 = 1.0 - damping * H2
C3 = H1 + H2 * (1.0 - damping * H1)
HH = H1 * H2


def swap_halves(a, b):
    axis = a.ndim - 2
    low = lax.broadcasted_iota(jnp.int32, a.shape, axis) < 4
    return (
        jnp.where(low, a, pltpu.roll(b, 4, axis)),
        jnp.where(low, pltpu.roll(a, 4, axis), b),
    )


def low_of_pairs(rows):
    tiles = rows.reshape(rows.shape[0] // 16, 2, 8, 128)
    return swap_halves(tiles[:, 0], tiles[:, 1])[0]


def pairs_of_low(chunks):
    low = lax.broadcasted_iota(jnp.int32, chunks.shape, 1) < 4
    first = jnp.where(low, chunks, 0.0)
    second = jnp.where(low, pltpu.roll(chunks, 4, 1), 0.0)
    return jnp.stack([first, second], axis=1).reshape(chunks.shape[0] * 16, 128)


def far_first(step, length):
    return lax.rem(length // 2 + length + (1 - 2 * lax.rem(step, 2)) * ((step + 1) // 2), length)


def dot(a, b, dims=(1, 0)):
    return lax.dot_general(
        a, b, (((dims[0],), (dims[1],)), ((), ())), preferred_element_type=F32
    )


def kernel(
    ns, nc, total_count,
    x_hbm, stiff_hbm, coef_hbm, slot_hbm, cl_hbm, cr_hbm, cm_hbm,
    st, growth_ref,
    xs, stiff, coef, slot, cl, cr, cm,
    keff, extra_k, mats, ends, picks, tabled,
    yp0, yp1, yp2, a0r, cross0, cross1, cross2,
    w_acc, p_acc, e1, e2p, e2w,
    send1, rcv1, send2, rcv2, send3, rcv3, send4, rcv4,
    nb_send, nb_rcv, nb_low, nb_low_rcv, acc1, acc2, part, colsum, secsum, secpart,
    load_sem, small_sem,
    nb_ssem, nb_rsem, a_ssem, a_rsem, r_ssem, r_rsem,
    low_ssem, low_rsem,
):
    me = lax.axis_index("sector")
    mycol = lax.axis_index("col")
    rows = xs.shape[1]
    cols = 2 * ns
    sectors = LOCAL * ns
    block = min(64, rows // 4)
    blocks = rows // block
    nxt = lax.rem(me + 1, ns)
    prv = lax.rem(me + ns - 1, ns)

    barrier = pltpu.get_barrier_semaphore()

    rings = ns // 4
    half = ns // 2
    wide = nc // 2
    core, along, high = lax.rem(me, 2), lax.rem(me // 2, rings), me // half
    across, lane = mycol // 2, lax.rem(mycol, 2)

    def peer(i):
        step, rest = far_first(i // 4, rings), lax.rem(i, 4)
        return (
            lax.rem(high + 1 - rest // 2, 2) * half
            + lax.rem(along + step, rings) * 2
            + lax.rem(core + 1 - lax.rem(rest, 2), 2)
        )

    def low_peer(i):
        step = far_first(i // 2, rings)
        return lax.rem(along + step, rings) * 2 + lax.rem(core + 1 - lax.rem(i, 2), 2)

    def high_peer(i):
        step, rest = far_first(i // 4, wide), lax.rem(i, 4)
        to = lax.rem(across + step, wide) * 2 + lax.rem(lane + 1 - lax.rem(rest, 2), 2)
        return lax.rem(high + 1 - rest // 2, 2), to

    def greet_sector(i, carry):
        pl.semaphore_signal(
            barrier, inc=1, device_id={"sector": peer(i)}, device_id_type=MESH
        )
        return carry

    def greet_other(i, carry):
        pl.semaphore_signal(
            barrier, inc=1,
            device_id={"sector": lax.rem(me + ns // 2, ns), "col": lax.rem(mycol + i, nc)},
            device_id_type=MESH,
        )
        return carry

    def greet_col(i, carry):
        pl.semaphore_signal(
            barrier, inc=1, device_id={"col": lax.rem(mycol + i, nc)}, device_id_type=MESH
        )
        return carry

    smalls = [
        pltpu.make_async_copy(src, dst, small_sem.at[n])
        for n, (src, dst) in enumerate(
            [(cl_hbm, cl), (cm_hbm, cm), (cr_hbm, cr), (stiff_hbm, stiff), (slot_hbm, slot)]
        )
    ]
    for copy in smalls:
        copy.start()
    quarter = rows // 4
    loads = [
        pltpu.make_async_copy(
            x_hbm.at[:, pl.ds(n * quarter, quarter), :],
            xs.at[:, pl.ds(n * quarter, quarter), :],
            load_sem.at[n],
        )
        for n in range(4)
    ]
    for copy in loads:
        copy.start()
    lax.fori_loop(0, ns - 1, greet_sector, 0)
    lax.fori_loop(1, nc, greet_other, 0)
    lax.fori_loop(1, nc, greet_col, 0)
    coef_load = pltpu.make_async_copy(coef_hbm, coef, load_sem.at[4])
    coef_load.start()

    def row_k(s):
        mask = cm[pl.ds(s, 1), :]
        return jnp.where(mask == 1, k_stick, jnp.where(mask == 2, k_slip, 0.0))

    for copy in smalls[0:4]:
        copy.wait()
    dof = lax.broadcasted_iota(jnp.int32, (DOF, 128), 0)
    mats_tri = jnp.where(
        jnp.abs(
            lax.broadcasted_iota(jnp.int32, (DOF, DOF), 0)
            - lax.broadcasted_iota(jnp.int32, (DOF, DOF), 1)
        )
        == 1,
        coupling,
        0.0,
    ).astype(BF16)
    eye = jnp.where(
        lax.broadcasted_iota(jnp.int32, (128, 128), 0)
        == lax.broadcasted_iota(jnp.int32, (128, 128), 1),
        1.0,
        0.0,
    ).astype(BF16)
    row8 = lax.broadcasted_iota(jnp.int32, (8, 128), 0)
    total_k = stiff[...]
    for s in range(LOCAL):
        k = row_k(s)
        left = cl[pl.ds(s, 1), :]
        right = cr[pl.ds(s, 1), :]
        at_left = jnp.where(dof == left, 1.0, 0.0).astype(BF16)
        at_right = jnp.where(dof == right, 1.0, 0.0).astype(BF16)
        more = dot(jnp.broadcast_to(k, (8, 128)).astype(BF16), at_left, (1, 1))
        if s > 0:
            mats[s - 1, 0:DOF, :] = dot(at_right, k_left, (1, 1)).astype(BF16)
            mats[s, DOF:2 * DOF, :] = dot(k_left, at_right, (1, 1)).astype(BF16)
            before = jnp.broadcast_to(row_k(s - 1), (8, 128)).astype(BF16)
            more = more + dot(before, at_right, (1, 1))
        else:
            ends[0] = at_right
            mats[0, DOF:DOF + 128, :] = dot(eye, at_right, (1, 1)).astype(BF16)
            mats[0, DOF + 128:2 * DOF, :] = jnp.zeros((128, DOF), BF16)
        if s == LOCAL - 1:
            ends[1] = at_left
            mats[s, 0:128, :] = dot(eye, at_left, (1, 1)).astype(BF16)
            mats[s, 128:DOF, :] = jnp.zeros((128, DOF), BF16)
        mats[s, 2 * DOF:3 * DOF, :] = mats_tri
        total_k = total_k + jnp.where(row8 == s, more[:, 0:128], 0.0)
        total_k = total_k + jnp.where(row8 == LOCAL + s, more[:, 128:256], 0.0)
        k_left = jnp.where(dof == left, jnp.broadcast_to(k, (DOF, 128)), 0.0).astype(BF16)
    keff[...] = total_k

    smalls[4].wait()
    smat = pltpu.roll(
        jnp.broadcast_to(slot[...].astype(F32), (sectors, sectors)), 0, 1, stride=1, stride_axis=0
    )
    for k in range(TABLES):
        picks[:, k * sectors:(k + 1) * sectors] = jnp.where(smat == float(k), 1.0, 0.0).astype(BF16)

    def combine(i, carry):
        at = pl.ds(pl.multiple_of(i * block, block), block)
        p = [xs[2 * j, at, :] for j in range(4)]
        w = [xs[2 * j + 1, at, :] for j in range(4)]

        def quad(m, v):
            out = v[0] * float(S[m][0])
            for j in range(1, 4):
                out = out + float(S[m][j]) * v[j]
            return out

        y0 = quad(0, p)
        v0 = quad(0, w)
        p1 = p[0] + v0
        y1 = quad(1, p) + H1 * (p1 - p[1])
        yp0[at, :] = y0
        yp1[at, :] = y1
        p_acc[at, :] = p1
        w_acc[at, :] = w[0] - damping * v0
        e1[at, :] = quad(1, w) - H1 * w[1]
        e2p[at, :] = quad(2, p) - H2 * p[2]
        e2w[at, :] = quad(2, w) - H2 * w[2]
        per = block // 16
        send1[pl.ds(i * per, per), :, 0:128] = low_of_pairs(y0).astype(BF16)
        send1[pl.ds(i * per, per), :, 128:256] = low_of_pairs(C3 * y0 + H2 * y1).astype(BF16)
        return carry

    for n in range(4):
        loads[n].wait()
        lax.fori_loop(n * blocks // 4, (n + 1) * blocks // 4, combine, 0)

    def sector_rows(ref, s):
        return jnp.concatenate(
            [ref[pl.ds(s, cols, stride=8), :], ref[pl.ds(4 + s, cols, stride=8), :]], axis=1
        )

    def neighbour_copies(field):
        return [
            pltpu.make_async_remote_copy(
                nb_send.at[side, field], nb_rcv.at[side, field],
                nb_ssem.at[side, field], nb_rsem.at[side, field],
                device_id={"sector": to}, device_id_type=MESH,
            )
            for side, to in ((0, prv), (1, nxt))
        ]

    def edge_rows(first, last):
        depth = first.shape[1]
        k = row_k(LOCAL - 1)
        return (
            dot(first, ends[0, 0:depth, :]).astype(BF16),
            (dot(last, ends[1, 0:depth, :]) * k).astype(BF16),
        )

    def fill_edges(field, ref):
        k = jnp.broadcast_to(row_k(LOCAL - 1), (16, 128)).astype(BF16)
        values = edge_rows(
            sector_rows(ref, 0).astype(BF16), sector_rows(ref, LOCAL - 1).astype(BF16)
        )
        for side in range(2):
            nb_send[side, field] = jnp.concatenate([values[side], k], axis=0)

    def from_edges(after, before):
        none = jnp.zeros((cols, 128), BF16)
        after = (after.astype(F32) * row_k(LOCAL - 1)).astype(BF16)
        return (
            jnp.concatenate([after, none], axis=1), jnp.concatenate([before, none], axis=1)
        )

    def send_all(src, dst, stage, ssem, rsem):
        def one(i, carry):
            to = peer(i)
            pltpu.make_async_remote_copy(
                src.at[to], dst.at[me], ssem.at[stage], rsem.at[stage],
                device_id={"sector": to}, device_id_type=MESH,
            ).start()
            return carry

        lax.fori_loop(0, ns - 1, one, 0)
        dst[me] = src[me]

    def wait_all(src, dst, stage, ssem, rsem):
        most = pl.ds(0, ns - 1)
        return pltpu.make_async_remote_copy(
            src.at[most], dst.at[most], ssem.at[stage], rsem.at[stage],
            device_id={"sector": nxt}, device_id_type=MESH,
        )

    fill_edges(0, yp0)
    edge0, edge1, edge2 = [neighbour_copies(field) for field in range(3)]

    pl.semaphore_wait(barrier, ns + 2 * nc - 3)

    for copy in edge0:
        copy.start()
    send_all(send1, rcv1, 0, a_ssem, a_rsem)

    def cross(own, next_first, prev_last, dst):
        chain = [prev_last] + own + [next_first]
        for s in range(LOCAL):
            lhs = jnp.concatenate([chain[s + 2], chain[s], chain[s + 1]], axis=1)
            out = dot(lhs, mats[s])
            dst[pl.ds(s, cols, stride=8), :] = out[:, 0:128]
            dst[pl.ds(4 + s, cols, stride=8), :] = out[:, 128:256]

    def edges_in(field):
        return from_edges(nb_rcv[0, field, 0:cols, :], nb_rcv[1, field, 0:cols, :])

    def fine_cross_of(field, ref, dst):
        none = jnp.zeros((cols, DOF), BF16)
        after, before = edges_in(field)
        chain = [jnp.concatenate([before, none], axis=0)]
        for s in range(LOCAL):
            value = sector_rows(ref, s)
            high = value.astype(BF16)
            chain.append(jnp.concatenate([high, (value - high.astype(F32)).astype(BF16)], axis=0))
        chain.append(jnp.concatenate([after, none], axis=0))
        for s in range(LOCAL):
            both = dot(jnp.concatenate([chain[s + 2], chain[s], chain[s + 1]], axis=1), mats[s])
            out = both[0:cols] + both[cols:2 * cols]
            dst[pl.ds(s, cols, stride=8), :] = out[:, 0:128]
            dst[pl.ds(4 + s, cols, stride=8), :] = out[:, 128:256]

    def times_k(rows_value):
        tiles = rows_value.reshape(rows_value.shape[0] // 8, 8, 128)
        return (tiles * keff[...][None]).reshape(rows_value.shape)

    none = jnp.zeros((cols, DOF), BF16)
    cross([sector_rows(yp0, s).astype(BF16) for s in range(LOCAL)], none, none, cross0)

    def second(i, carry):
        at = pl.ds(pl.multiple_of(i * block, block), block)
        y0 = yp0[at, :]
        w1 = w_acc[at, :] + cross0[at, :] - times_k(y0)
        v1 = H1 * w1 + e1[at, :]
        p2 = p_acc[at, :] + v1
        y2 = H2 * p2 + e2p[at, :]
        yp2[at, :] = y2
        p_acc[at, :] = p2
        w_acc[at, :] = w1 - damping * v1
        cross1[at, :] = C1 * y0 + C2 * yp1[at, :] + y2
        return carry

    lax.fori_loop(0, blocks, second, 0)

    for copy in edge0:
        copy.wait()
    after, before = edges_in(0)
    out = dot(before[:, 0:128], mats[0, DOF:DOF + 128, :])
    cross0[pl.ds(0, cols, stride=8), :] = out[:, 0:128]
    cross0[pl.ds(4, cols, stride=8), :] = out[:, 128:256]
    out = dot(after[:, 0:128], mats[LOCAL - 1, 0:128, :])
    cross0[pl.ds(LOCAL - 1, cols, stride=8), :] = out[:, 0:128]
    cross0[pl.ds(4 + LOCAL - 1, cols, stride=8), :] = out[:, 128:256]
    more = dot(nb_rcv[1, 0, cols:cols + 16, :], ends[0], (1, 1))[0:8]
    extra_k[...] = jnp.where(row8 == 0, more[:, 0:128], 0.0) + jnp.where(
        row8 == LOCAL, more[:, 128:256], 0.0
    )
    place = lax.broadcasted_iota(jnp.int32, (block // 8, 8, 128), 1) % LOCAL
    outer = (place == 0) | (place == LOCAL - 1)

    def correction(at):
        shape = (block // 8, 8, 128)
        value = jnp.where(outer, cross0[at, :].reshape(shape), 0.0)
        return (value - extra_k[...][None] * yp0[at, :].reshape(shape)).reshape(block, 128)

    def correct_v(i, carry):
        at = pl.ds(pl.multiple_of(i * block, block), block)
        per = block // 16
        send2[pl.ds(i * per, per)] = low_of_pairs(cross1[at, :] + HH * correction(at)).astype(BF16)
        return carry

    lax.fori_loop(0, blocks, correct_v, 0)
    send_all(send2, rcv2, 1, a_ssem, a_rsem)

    def correct_rest(i, carry):
        at = pl.ds(pl.multiple_of(i * block, block), block)
        change = correction(at)
        yp2[at, :] = yp2[at, :] + HH * change
        p_acc[at, :] = p_acc[at, :] + H1 * change
        w_acc[at, :] = w_acc[at, :] + (1.0 - damping * H1) * change
        return carry

    lax.fori_loop(0, blocks, correct_rest, 0)
    keff[...] = keff[...] + extra_k[...]
    fill_edges(1, yp1)
    fill_edges(2, yp2)
    for copy in edge1 + edge2:
        copy.start()

    coef_load.wait()

    def loads_of(surfaces, acc):
        parts = len(surfaces)
        lhs = jnp.concatenate(list(surfaces), axis=0).astype(BF16)
        for k in range(0, TABLES, 2):
            u = dot(lhs, coef[k * AERO:(k + 2) * AERO, :], (1, 1)).astype(BF16)
            for n in range(2):
                for c in range(parts):
                    tabled[
                        (k + n) * sectors:(k + n + 1) * sectors, c * AERO:(c + 1) * AERO
                    ] = u[c * sectors:(c + 1) * sectors, n * AERO:(n + 1) * AERO]
        acc[...] = dot(picks[...], tabled[:, 0:parts * AERO])

    def by_sector(received):
        value = received.astype(F32).reshape(ns // 2, 2, 8, received.shape[2])
        first, second_ = swap_halves(value[:, 0], value[:, 1])
        return first.reshape(sectors, -1), second_.reshape(sectors, -1)

    def by_device(first, second_):
        lo, hi = swap_halves(
            first.reshape(ns // 2, 8, 128), second_.reshape(ns // 2, 8, 128)
        )
        return jnp.stack([lo, hi], axis=1).reshape(ns, 8, 128)

    wait_all(send1, rcv1, 0, a_ssem, a_rsem).wait()
    arrived = by_sector(rcv1[...])
    loads_of([arrived[c][:, f * AERO:(f + 1) * AERO] for f in range(2) for c in range(2)], acc2)
    for n in range(2):
        at = 2 * n * AERO
        send3[:, :, n * AERO:(n + 1) * AERO] = by_device(
            acc2[:, at:at + AERO], acc2[:, at + AERO:at + 2 * AERO]
        ).astype(BF16)
    send_all(send3, rcv3, 0, r_ssem, r_rsem)

    wait_all(send2, rcv2, 1, a_ssem, a_rsem).wait()
    rest = by_sector(rcv2[...])
    loads_of([rest[c] + HH * acc2[:, c * AERO:(c + 1) * AERO] for c in range(2)], acc1)
    send4[...] = by_device(acc1[:, 0:AERO], acc1[:, AERO:2 * AERO]).astype(BF16)
    send_all(send4, rcv4, 1, r_ssem, r_rsem)

    for copy in edge1 + edge2:
        copy.wait()
    fine_cross_of(1, yp1, cross1)
    fine_cross_of(2, yp2, cross2)

    def third(i, carry):
        at = pl.ds(pl.multiple_of(i * block, block), block)
        w2 = w_acc[at, :] + cross1[at, :] - times_k(yp1[at, :])
        v2 = H2 * w2 + e2w[at, :]
        p_acc[at, :] = p_acc[at, :] + v2
        w_acc[at, :] = w2 - damping * v2 + cross2[at, :] - times_k(yp2[at, :])
        return carry

    lax.fori_loop(0, blocks, third, 0)

    wait_all(send3, rcv3, 0, r_ssem, r_rsem).wait()

    def spread(i, carry):
        per = block // 16
        at = pl.ds(pl.multiple_of(i * block, block), block)
        got = rcv3[pl.ds(i * per, per)].astype(F32)
        a0r[at, :] = pairs_of_low(got[:, :, 0:128])
        p3 = p_acc[at, :] + pairs_of_low(got[:, :, 128:256])
        st[0, at, :] = p3
        return carry + jnp.sum((p3 * p3).reshape(block // 8, 8, 128), axis=0)

    squares = lax.fori_loop(0, blocks, spread, jnp.zeros((8, 128), F32))

    none = jnp.zeros((cols, 128), BF16)
    own = [a0r[pl.ds(s, cols, stride=8), :].astype(BF16) for s in range(LOCAL)]
    nb_low[0], nb_low[1] = edge_rows(own[0], own[LOCAL - 1])
    edge_low = [
        pltpu.make_async_remote_copy(
            nb_low.at[side], nb_low_rcv.at[side], low_ssem.at[side], low_rsem.at[side],
            device_id={"sector": to}, device_id_type=MESH,
        )
        for side, to in ((0, prv), (1, nxt))
    ]
    for copy in edge_low:
        copy.start()

    for copy in edge_low:
        copy.wait()
    cross(
        [jnp.concatenate([v, none], axis=1) for v in own],
        *from_edges(nb_low_rcv[0], nb_low_rcv[1]),
        cross0,
    )

    def fourth(i, carry):
        at = pl.ds(pl.multiple_of(i * block, block), block)
        w_acc[at, :] = w_acc[at, :] + HH * (cross0[at, :] - times_k(a0r[at, :]))
        return carry

    lax.fori_loop(0, blocks, fourth, 0)

    wait_all(send4, rcv4, 1, r_ssem, r_rsem).wait()

    def close(i, carry):
        per = block // 16
        at = pl.ds(pl.multiple_of(i * block, block), block)
        w3 = w_acc[at, :] + pairs_of_low(rcv4[pl.ds(i * per, per)].astype(F32))
        st[1, at, :] = w3
        return carry + jnp.sum((w3 * w3).reshape(block // 8, 8, 128), axis=0)

    squares = lax.fori_loop(0, blocks, close, squares)

    part[...] = jnp.sum(squares, axis=0, keepdims=True)

    low = lax.rem(me, half)
    spot = high * nc + mycol

    def over_low(i, carry):
        to = low_peer(i)
        pltpu.make_async_remote_copy(
            part, secsum.at[low], r_ssem.at[2], r_rsem.at[2],
            device_id={"sector": high * half + to}, device_id_type=MESH,
        ).start()
        return carry

    lax.fori_loop(0, half - 1, over_low, 0)
    secsum[low] = part[...]
    most_low = pl.ds(0, half - 1)
    pltpu.make_async_remote_copy(
        secsum.at[most_low], secsum.at[most_low], r_ssem.at[2], r_rsem.at[2],
        device_id={"sector": nxt}, device_id_type=MESH,
    ).wait()
    secpart[...] = jnp.sum(secsum[...], axis=0)

    def over_high(i, carry):
        to_high, to = high_peer(i)
        pltpu.make_async_remote_copy(
            secpart, colsum.at[spot], a_ssem.at[2], a_rsem.at[2],
            device_id={"sector": low + half * to_high, "col": to},
            device_id_type=MESH,
        ).start()
        return carry

    lax.fori_loop(0, 2 * nc - 1, over_high, 0)
    colsum[spot] = secpart[...]
    most = pl.ds(0, 2 * nc - 1)
    pltpu.make_async_remote_copy(
        colsum.at[most], colsum.at[most], a_ssem.at[2], a_rsem.at[2],
        device_id={"sector": nxt}, device_id_type=MESH,
    ).wait()
    everything = jnp.sum(jnp.sum(colsum[...], axis=0), axis=1, keepdims=True)
    growth_ref[...] = jnp.broadcast_to(jnp.sqrt(everything / total_count + 1e-6), (1, 128))


def per_device(
    ns, nc, prev_nodes, stiffness, aero_coef, offset_slot, contact_left, contact_right, contact_mask
):
    cols = prev_nodes.shape[2]
    rows = cols * 8
    sectors = ns * LOCAL
    x = prev_nodes.reshape(8, cols, LOCAL, 2, 128).transpose(0, 1, 3, 2, 4).reshape(8, rows, 128)
    stiff = stiffness.reshape(LOCAL, 2, 128).transpose(1, 0, 2).reshape(8, 128)
    vm = pltpu.VMEM
    big = vm((rows, 128), F32)
    ints = vm((LOCAL, 128), jnp.int32)
    dma = pltpu.SemaphoreType.DMA
    any_spec = pl.BlockSpec(memory_space=pl.ANY)
    state, growth = pl.pallas_call(
        functools.partial(kernel, ns, nc, float(2 * cols * nc * sectors * DOF)),
        out_shape=(
            pltpu.VMEM((2, rows, 128), F32),
            pltpu.VMEM((1, 128), F32),
        ),
        in_specs=[any_spec] * 7,
        out_specs=(pl.BlockSpec(memory_space=pltpu.VMEM), pl.BlockSpec(memory_space=pltpu.VMEM)),
        scratch_shapes=[
            vm((8, rows, 128), F32),
            vm((8, 128), F32),
            vm((TABLES * AERO, AERO), BF16),
            vm((1, sectors), jnp.int32),
            ints, ints, ints,
            vm((8, 128), F32),
            vm((8, 128), F32),
            vm((LOCAL, 3 * DOF, DOF), BF16),
            vm((2, DOF, 128), BF16),
            vm((sectors, TABLES * sectors), BF16),
            vm((TABLES * sectors, 4 * AERO), BF16),
            big, big, big, big, big, big, big,
            big, big, big, big, big,
            vm((ns, 8, 256), BF16), vm((ns, 8, 256), BF16),
            vm((ns, 8, 128), BF16), vm((ns, 8, 128), BF16),
            vm((ns, 8, 256), BF16), vm((ns, 8, 256), BF16),
            vm((ns, 8, 128), BF16), vm((ns, 8, 128), BF16),
            vm((2, 3, cols + 16, 128), BF16), vm((2, 3, cols + 16, 128), BF16),
            vm((2, cols, 128), BF16), vm((2, cols, 128), BF16),
            vm((sectors, 2 * AERO), F32),
            vm((sectors, 4 * AERO), F32),
            vm((1, 128), F32),
            vm((2 * nc, 1, 128), F32),
            vm((ns // 2, 1, 128), F32),
            vm((1, 128), F32),
            dma((5,)), dma((5,)),
            dma((2, 3)), dma((2, 3)),
            dma((3,)), dma((3,)), dma((3,)), dma((3,)),
            dma((2,)), dma((2,)),
        ],
        compiler_params=pltpu.CompilerParams(
            collective_id=0, has_side_effects=True, vmem_limit_bytes=60 << 20
        ),
        name="sweep",
    )(
        x, stiff, aero_coef.reshape(TABLES * AERO, AERO), offset_slot.reshape(1, sectors),
        contact_left, contact_right, contact_mask,
    )
    value = growth[0, 0]
    scaled = state / value
    scaled = scaled.reshape(2, cols, 2, LOCAL, 128).transpose(0, 1, 3, 2, 4)
    return scaled.reshape(2, cols, LOCAL, DOF), value


def solution(mesh):
    ns, nc = mesh.shape["sector"], mesh.shape["col"]
    placed = (
        P(None, None, "col", "sector", None),
        P("sector", None),
        P(),
        P(),
        P("sector", None),
        P("sector", None),
        P("sector", None),
    )
    return jax.shard_map(
        functools.partial(per_device, ns, nc),
        mesh=mesh,
        in_specs=placed,
        out_specs=(P(None, "col", "sector", None), P()),
        check_vma=False,
    )
```

```python
import functools
import math

import jax
import jax.numpy as jnp
from jax import lax
from jax.experimental import pallas as pl
from jax.experimental.pallas import tpu as pltpu
from jax.sharding import PartitionSpec as P

DOF = 256
AERO = 128
TABLES = 32
LOCAL = 4
MESH = pl.DeviceIdType.MESH
F32 = jnp.float32
BF16 = jnp.bfloat16

time_step = 0.25
coupling = 0.5
damping = 0.1
k_stick = 4.0
k_slip = 1.0


def quad_tables():
    root = 1.0 / math.sqrt(5.0)
    tau = [0.0, (1.0 - root) / 2.0, (1.0 + root) / 2.0, 1.0]
    table = []
    for m in range(3):
        table_row = []
        for j in range(4):
            coeffs = [1.0]
            scale = 1.0
            for k in range(4):
                if k != j:
                    widened = [0.0] * (len(coeffs) + 1)
                    for power in range(len(coeffs)):
                        widened[power + 1] = widened[power + 1] + coeffs[power]
                        widened[power] = widened[power] - tau[k] * coeffs[power]
                    coeffs = widened
                    scale = scale * (tau[j] - tau[k])
            integral = 0.0
            for power in range(len(coeffs)):
                integral = integral + coeffs[power] * (
                    tau[m + 1] ** (power + 1) - tau[m] ** (power + 1)
                ) / (power + 1)
            table_row.append(integral / scale * time_step)
        table.append(table_row)
    steps = [(tau[m + 1] - tau[m]) * time_step for m in range(3)]
    return (table, steps)


S, H = quad_tables()
H1, H2 = H[1], H[2]
C1 = (1.0 - damping * H1) * (1.0 - damping * H2)
C2 = 1.0 - damping * H2
C3 = H1 + H2 * (1.0 - damping * H1)
HH = H1 * H2


def swap_halves(a, b):
    axis = a.ndim - 2
    low = lax.broadcasted_iota(jnp.int32, a.shape, axis) < 4
    return (
        jnp.where(low, a, pltpu.roll(b, 4, axis)),
        jnp.where(low, pltpu.roll(a, 4, axis), b),
    )


def low_of_pairs(rows):
    tiles = rows.reshape(rows.shape[0] // 16, 2, 8, 128)
    return swap_halves(tiles[:, 0], tiles[:, 1])[0]


def pairs_of_low(chunks):
    low = lax.broadcasted_iota(jnp.int32, chunks.shape, 1) < 4
    first = jnp.where(low, chunks, 0.0)
    second = jnp.where(low, pltpu.roll(chunks, 4, 1), 0.0)
    return jnp.stack([first, second], axis=1).reshape(chunks.shape[0] * 16, 128)


def far_first(step, length):
    return lax.rem(length // 2 + length + (1 - 2 * lax.rem(step, 2)) * ((step + 1) // 2), length)


def dot(a, b, dims=(1, 0)):
    return lax.dot_general(
        a, b, (((dims[0],), (dims[1],)), ((), ())), preferred_element_type=F32
    )


def kernel(
    ns, nc, total_count,
    x_hbm, stiff_hbm, coef_hbm, slot_hbm, cl_hbm, cr_hbm, cm_hbm,
    st, growth_ref,
    xs, stiff, coef, slot, cl, cr, cm,
    keff, extra_k, mats, ends, picks, tabled,
    yp0, yp1, yp2, a0r, cross0, cross1, cross2,
    w_acc, p_acc, e1, e2p, e2w,
    send1, rcv1, send2, rcv2, send3, rcv3, send4, rcv4,
    nb_send, nb_rcv, nb_low, nb_low_rcv, acc1, acc2, part, colsum, secsum, secpart,
    load_sem, small_sem,
    nb_ssem, nb_rsem, a_ssem, a_rsem, r_ssem, r_rsem,
    low_ssem, low_rsem,
):
    me = lax.axis_index("sector")
    mycol = lax.axis_index("col")
    rows = xs.shape[1]
    cols = 2 * ns
    sectors = LOCAL * ns
    block = min(64, rows // 4)
    blocks = rows // block
    nxt = lax.rem(me + 1, ns)
    prv = lax.rem(me + ns - 1, ns)

    barrier = pltpu.get_barrier_semaphore()

    rings = ns // 4
    half = ns // 2
    wide = nc // 2
    core, along, high = lax.rem(me, 2), lax.rem(me // 2, rings), me // half
    across, lane = mycol // 2, lax.rem(mycol, 2)

    def peer(i):
        step, rest = far_first(i // 4, rings), lax.rem(i, 4)
        return (
            lax.rem(high + 1 - rest // 2, 2) * half
            + lax.rem(along + step, rings) * 2
            + lax.rem(core + 1 - lax.rem(rest, 2), 2)
        )

    def low_peer(i):
        step = far_first(i // 2, rings)
        return lax.rem(along + step, rings) * 2 + lax.rem(core + 1 - lax.rem(i, 2), 2)

    def high_peer(i):
        step, rest = far_first(i // 4, wide), lax.rem(i, 4)
        to = lax.rem(across + step, wide) * 2 + lax.rem(lane + 1 - lax.rem(rest, 2), 2)
        return lax.rem(high + 1 - rest // 2, 2), to

    def greet_sector(i, carry):
        pl.semaphore_signal(
            barrier, inc=1, device_id={"sector": peer(i)}, device_id_type=MESH
        )
        return carry

    def greet_other(i, carry):
        pl.semaphore_signal(
            barrier, inc=1,
            device_id={"sector": lax.rem(me + ns // 2, ns), "col": lax.rem(mycol + i, nc)},
            device_id_type=MESH,
        )
        return carry

    def greet_col(i, carry):
        pl.semaphore_signal(
            barrier, inc=1, device_id={"col": lax.rem(mycol + i, nc)}, device_id_type=MESH
        )
        return carry

    smalls = [
        pltpu.make_async_copy(src, dst, small_sem.at[n])
        for n, (src, dst) in enumerate(
            [(cl_hbm, cl), (cm_hbm, cm), (cr_hbm, cr), (stiff_hbm, stiff), (slot_hbm, slot)]
        )
    ]
    for copy in smalls:
        copy.start()
    quarter = rows // 4
    loads = [
        pltpu.make_async_copy(
            x_hbm.at[:, pl.ds(n * quarter, quarter), :],
            xs.at[:, pl.ds(n * quarter, quarter), :],
            load_sem.at[n],
        )
        for n in range(4)
    ]
    for copy in loads:
        copy.start()
    lax.fori_loop(0, ns - 1, greet_sector, 0, unroll=True)
    lax.fori_loop(1, nc, greet_other, 0)
    lax.fori_loop(1, nc, greet_col, 0)
    coef_load = pltpu.make_async_copy(coef_hbm, coef, load_sem.at[4])
    coef_load.start()

    def row_k(s):
        mask = cm[pl.ds(s, 1), :]
        return jnp.where(mask == 1, k_stick, jnp.where(mask == 2, k_slip, 0.0))

    for copy in smalls[0:4]:
        copy.wait()
    dof = lax.broadcasted_iota(jnp.int32, (DOF, 128), 0)
    mats_tri = jnp.where(
        jnp.abs(
            lax.broadcasted_iota(jnp.int32, (DOF, DOF), 0)
            - lax.broadcasted_iota(jnp.int32, (DOF, DOF), 1)
        )
        == 1,
        coupling,
        0.0,
    ).astype(BF16)
    eye = jnp.where(
        lax.broadcasted_iota(jnp.int32, (128, 128), 0)
        == lax.broadcasted_iota(jnp.int32, (128, 128), 1),
        1.0,
        0.0,
    ).astype(BF16)
    row8 = lax.broadcasted_iota(jnp.int32, (8, 128), 0)
    total_k = stiff[...]
    for s in range(LOCAL):
        k = row_k(s)
        left = cl[pl.ds(s, 1), :]
        right = cr[pl.ds(s, 1), :]
        at_left = jnp.where(dof == left, 1.0, 0.0).astype(BF16)
        at_right = jnp.where(dof == right, 1.0, 0.0).astype(BF16)
        more = dot(jnp.broadcast_to(k, (8, 128)).astype(BF16), at_left, (1, 1))
        if s > 0:
            mats[s - 1, 0:DOF, :] = dot(at_right, k_left, (1, 1)).astype(BF16)
            mats[s, DOF:2 * DOF, :] = dot(k_left, at_right, (1, 1)).astype(BF16)
            before = jnp.broadcast_to(row_k(s - 1), (8, 128)).astype(BF16)
            more = more + dot(before, at_right, (1, 1))
        else:
            ends[0] = at_right
            mats[0, DOF:DOF + 128, :] = dot(eye, at_right, (1, 1)).astype(BF16)
            mats[0, DOF + 128:2 * DOF, :] = jnp.zeros((128, DOF), BF16)
        if s == LOCAL - 1:
            ends[1] = at_left
            mats[s, 0:128, :] = dot(eye, at_left, (1, 1)).astype(BF16)
            mats[s, 128:DOF, :] = jnp.zeros((128, DOF), BF16)
        mats[s, 2 * DOF:3 * DOF, :] = mats_tri
        total_k = total_k + jnp.where(row8 == s, more[:, 0:128], 0.0)
        total_k = total_k + jnp.where(row8 == LOCAL + s, more[:, 128:256], 0.0)
        k_left = jnp.where(dof == left, jnp.broadcast_to(k, (DOF, 128)), 0.0).astype(BF16)
    keff[...] = total_k

    smalls[4].wait()
    smat = pltpu.roll(
        jnp.broadcast_to(slot[...].astype(F32), (sectors, sectors)), 0, 1, stride=1, stride_axis=0
    )
    for k in range(TABLES):
        picks[:, k * sectors:(k + 1) * sectors] = jnp.where(smat == float(k), 1.0, 0.0).astype(BF16)

    def combine(i, carry):
        at = pl.ds(pl.multiple_of(i * block, block), block)
        p = [xs[2 * j, at, :] for j in range(4)]
        w = [xs[2 * j + 1, at, :] for j in range(4)]

        def quad(m, v):
            out = v[0] * float(S[m][0])
            for j in range(1, 4):
                out = out + float(S[m][j]) * v[j]
            return out

        y0 = quad(0, p)
        v0 = quad(0, w)
        p1 = p[0] + v0
        y1 = quad(1, p) + H1 * (p1 - p[1])
        yp0[at, :] = y0
        yp1[at, :] = y1
        p_acc[at, :] = p1
        w_acc[at, :] = w[0] - damping * v0
        e1[at, :] = quad(1, w) - H1 * w[1]
        e2p[at, :] = quad(2, p) - H2 * p[2]
        e2w[at, :] = quad(2, w) - H2 * w[2]
        per = block // 16
        send1[pl.ds(i * per, per), :, 0:128] = low_of_pairs(y0).astype(BF16)
        send1[pl.ds(i * per, per), :, 128:256] = low_of_pairs(C3 * y0 + H2 * y1).astype(BF16)
        return carry

    for n in range(4):
        loads[n].wait()
        lax.fori_loop(n * blocks // 4, (n + 1) * blocks // 4, combine, 0)

    def sector_rows(ref, s):
        return jnp.concatenate(
            [ref[pl.ds(s, cols, stride=8), :], ref[pl.ds(4 + s, cols, stride=8), :]], axis=1
        )

    def neighbour_copies(field):
        return [
            pltpu.make_async_remote_copy(
                nb_send.at[side, field], nb_rcv.at[side, field],
                nb_ssem.at[side, field], nb_rsem.at[side, field],
                device_id={"sector": to}, device_id_type=MESH,
            )
            for side, to in ((0, prv), (1, nxt))
        ]

    def edge_rows(first, last):
        depth = first.shape[1]
        k = row_k(LOCAL - 1)
        return (
            dot(first, ends[0, 0:depth, :]).astype(BF16),
            (dot(last, ends[1, 0:depth, :]) * k).astype(BF16),
        )

    def fill_edges(field, ref):
        k = jnp.broadcast_to(row_k(LOCAL - 1), (16, 128)).astype(BF16)
        values = edge_rows(
            sector_rows(ref, 0).astype(BF16), sector_rows(ref, LOCAL - 1).astype(BF16)
        )
        for side in range(2):
            nb_send[side, field] = jnp.concatenate([values[side], k], axis=0)

    def from_edges(after, before):
        none = jnp.zeros((cols, 128), BF16)
        after = (after.astype(F32) * row_k(LOCAL - 1)).astype(BF16)
        return (
            jnp.concatenate([after, none], axis=1), jnp.concatenate([before, none], axis=1)
        )

    def send_all(src, dst, stage, ssem, rsem):
        def one(i, carry):
            to = peer(i)
            pltpu.make_async_remote_copy(
                src.at[to], dst.at[me], ssem.at[stage], rsem.at[stage],
                device_id={"sector": to}, device_id_type=MESH,
            ).start()
            return carry

        lax.fori_loop(0, ns - 1, one, 0, unroll=True)
        dst[me] = src[me]

    def wait_all(src, dst, stage, ssem, rsem):
        most = pl.ds(0, ns - 1)
        return pltpu.make_async_remote_copy(
            src.at[most], dst.at[most], ssem.at[stage], rsem.at[stage],
            device_id={"sector": nxt}, device_id_type=MESH,
        )

    fill_edges(0, yp0)
    edge0, edge1, edge2 = [neighbour_copies(field) for field in range(3)]

    pl.semaphore_wait(barrier, ns + 2 * nc - 3)

    for copy in edge0:
        copy.start()
    send_all(send1, rcv1, 0, a_ssem, a_rsem)

    def cross(own, next_first, prev_last, dst):
        chain = [prev_last] + own + [next_first]
        for s in range(LOCAL):
            lhs = jnp.concatenate([chain[s + 2], chain[s], chain[s + 1]], axis=1)
            out = dot(lhs, mats[s])
            dst[pl.ds(s, cols, stride=8), :] = out[:, 0:128]
            dst[pl.ds(4 + s, cols, stride=8), :] = out[:, 128:256]

    def edges_in(field):
        return from_edges(nb_rcv[0, field, 0:cols, :], nb_rcv[1, field, 0:cols, :])

    def fine_cross_of(field, ref, dst):
        none = jnp.zeros((cols, DOF), BF16)
        after, before = edges_in(field)
        chain = [jnp.concatenate([before, none], axis=0)]
        for s in range(LOCAL):
            value = sector_rows(ref, s)
            high = value.astype(BF16)
            chain.append(jnp.concatenate([high, (value - high.astype(F32)).astype(BF16)], axis=0))
        chain.append(jnp.concatenate([after, none], axis=0))
        for s in range(LOCAL):
            both = dot(jnp.concatenate([chain[s + 2], chain[s], chain[s + 1]], axis=1), mats[s])
            out = both[0:cols] + both[cols:2 * cols]
            dst[pl.ds(s, cols, stride=8), :] = out[:, 0:128]
            dst[pl.ds(4 + s, cols, stride=8), :] = out[:, 128:256]

    def times_k(rows_value):
        tiles = rows_value.reshape(rows_value.shape[0] // 8, 8, 128)
        return (tiles * keff[...][None]).reshape(rows_value.shape)

    none = jnp.zeros((cols, DOF), BF16)
    cross([sector_rows(yp0, s).astype(BF16) for s in range(LOCAL)], none, none, cross0)

    def second(i, carry):
        at = pl.ds(pl.multiple_of(i * block, block), block)
        y0 = yp0[at, :]
        w1 = w_acc[at, :] + cross0[at, :] - times_k(y0)
        v1 = H1 * w1 + e1[at, :]
        p2 = p_acc[at, :] + v1
        y2 = H2 * p2 + e2p[at, :]
        yp2[at, :] = y2
        p_acc[at, :] = p2
        w_acc[at, :] = w1 - damping * v1
        cross1[at, :] = C1 * y0 + C2 * yp1[at, :] + y2
        return carry

    lax.fori_loop(0, blocks, second, 0)

    for copy in edge0:
        copy.wait()
    after, before = edges_in(0)
    out = dot(before[:, 0:128], mats[0, DOF:DOF + 128, :])
    cross0[pl.ds(0, cols, stride=8), :] = out[:, 0:128]
    cross0[pl.ds(4, cols, stride=8), :] = out[:, 128:256]
    out = dot(after[:, 0:128], mats[LOCAL - 1, 0:128, :])
    cross0[pl.ds(LOCAL - 1, cols, stride=8), :] = out[:, 0:128]
    cross0[pl.ds(4 + LOCAL - 1, cols, stride=8), :] = out[:, 128:256]
    more = dot(nb_rcv[1, 0, cols:cols + 16, :], ends[0], (1, 1))[0:8]
    extra_k[...] = jnp.where(row8 == 0, more[:, 0:128], 0.0) + jnp.where(
        row8 == LOCAL, more[:, 128:256], 0.0
    )
    place = lax.broadcasted_iota(jnp.int32, (block // 8, 8, 128), 1) % LOCAL
    outer = (place == 0) | (place == LOCAL - 1)

    def correction(at):
        shape = (block // 8, 8, 128)
        value = jnp.where(outer, cross0[at, :].reshape(shape), 0.0)
        return (value - extra_k[...][None] * yp0[at, :].reshape(shape)).reshape(block, 128)

    def correct_v(i, carry):
        at = pl.ds(pl.multiple_of(i * block, block), block)
        per = block // 16
        send2[pl.ds(i * per, per)] = low_of_pairs(cross1[at, :] + HH * correction(at)).astype(BF16)
        return carry

    lax.fori_loop(0, blocks, correct_v, 0)
    send_all(send2, rcv2, 1, a_ssem, a_rsem)

    def correct_rest(i, carry):
        at = pl.ds(pl.multiple_of(i * block, block), block)
        change = correction(at)
        yp2[at, :] = yp2[at, :] + HH * change
        p_acc[at, :] = p_acc[at, :] + H1 * change
        w_acc[at, :] = w_acc[at, :] + (1.0 - damping * H1) * change
        return carry

    lax.fori_loop(0, blocks, correct_rest, 0)
    keff[...] = keff[...] + extra_k[...]
    fill_edges(1, yp1)
    fill_edges(2, yp2)
    for copy in edge1 + edge2:
        copy.start()

    coef_load.wait()

    def loads_of(surfaces, acc):
        parts = len(surfaces)
        lhs = jnp.concatenate(list(surfaces), axis=0).astype(BF16)
        for k in range(0, TABLES, 2):
            u = dot(lhs, coef[k * AERO:(k + 2) * AERO, :], (1, 1)).astype(BF16)
            for n in range(2):
                for c in range(parts):
                    tabled[
                        (k + n) * sectors:(k + n + 1) * sectors, c * AERO:(c + 1) * AERO
                    ] = u[c * sectors:(c + 1) * sectors, n * AERO:(n + 1) * AERO]
        acc[...] = dot(picks[...], tabled[:, 0:parts * AERO])

    def by_sector(received):
        value = received.astype(F32).reshape(ns // 2, 2, 8, received.shape[2])
        first, second_ = swap_halves(value[:, 0], value[:, 1])
        return first.reshape(sectors, -1), second_.reshape(sectors, -1)

    def by_device(first, second_):
        lo, hi = swap_halves(
            first.reshape(ns // 2, 8, 128), second_.reshape(ns // 2, 8, 128)
        )
        return jnp.stack([lo, hi], axis=1).reshape(ns, 8, 128)

    wait_all(send1, rcv1, 0, a_ssem, a_rsem).wait()
    arrived = by_sector(rcv1[...])
    loads_of([arrived[c][:, f * AERO:(f + 1) * AERO] for f in range(2) for c in range(2)], acc2)
    for n in range(2):
        at = 2 * n * AERO
        send3[:, :, n * AERO:(n + 1) * AERO] = by_device(
            acc2[:, at:at + AERO], acc2[:, at + AERO:at + 2 * AERO]
        ).astype(BF16)
    send_all(send3, rcv3, 0, r_ssem, r_rsem)

    wait_all(send2, rcv2, 1, a_ssem, a_rsem).wait()
    rest = by_sector(rcv2[...])
    loads_of([rest[c] + HH * acc2[:, c * AERO:(c + 1) * AERO] for c in range(2)], acc1)
    send4[...] = by_device(acc1[:, 0:AERO], acc1[:, AERO:2 * AERO]).astype(BF16)
    send_all(send4, rcv4, 1, r_ssem, r_rsem)

    for copy in edge1 + edge2:
        copy.wait()
    fine_cross_of(1, yp1, cross1)
    fine_cross_of(2, yp2, cross2)

    def third(i, carry):
        at = pl.ds(pl.multiple_of(i * block, block), block)
        w2 = w_acc[at, :] + cross1[at, :] - times_k(yp1[at, :])
        v2 = H2 * w2 + e2w[at, :]
        p_acc[at, :] = p_acc[at, :] + v2
        w_acc[at, :] = w2 - damping * v2 + cross2[at, :] - times_k(yp2[at, :])
        return carry

    lax.fori_loop(0, blocks, third, 0)

    wait_all(send3, rcv3, 0, r_ssem, r_rsem).wait()

    def spread(i, carry):
        per = block // 16
        at = pl.ds(pl.multiple_of(i * block, block), block)
        got = rcv3[pl.ds(i * per, per)].astype(F32)
        a0r[at, :] = pairs_of_low(got[:, :, 0:128])
        p3 = p_acc[at, :] + pairs_of_low(got[:, :, 128:256])
        st[0, at, :] = p3
        return carry + jnp.sum((p3 * p3).reshape(block // 8, 8, 128), axis=0)

    squares = lax.fori_loop(0, blocks, spread, jnp.zeros((8, 128), F32))

    none = jnp.zeros((cols, 128), BF16)
    own = [a0r[pl.ds(s, cols, stride=8), :].astype(BF16) for s in range(LOCAL)]
    nb_low[0], nb_low[1] = edge_rows(own[0], own[LOCAL - 1])
    edge_low = [
        pltpu.make_async_remote_copy(
            nb_low.at[side], nb_low_rcv.at[side], low_ssem.at[side], low_rsem.at[side],
            device_id={"sector": to}, device_id_type=MESH,
        )
        for side, to in ((0, prv), (1, nxt))
    ]
    for copy in edge_low:
        copy.start()

    for copy in edge_low:
        copy.wait()
    cross(
        [jnp.concatenate([v, none], axis=1) for v in own],
        *from_edges(nb_low_rcv[0], nb_low_rcv[1]),
        cross0,
    )

    def fourth(i, carry):
        at = pl.ds(pl.multiple_of(i * block, block), block)
        w_acc[at, :] = w_acc[at, :] + HH * (cross0[at, :] - times_k(a0r[at, :]))
        return carry

    lax.fori_loop(0, blocks, fourth, 0)

    wait_all(send4, rcv4, 1, r_ssem, r_rsem).wait()

    def close(i, carry):
        per = block // 16
        at = pl.ds(pl.multiple_of(i * block, block), block)
        w3 = w_acc[at, :] + pairs_of_low(rcv4[pl.ds(i * per, per)].astype(F32))
        st[1, at, :] = w3
        return carry + jnp.sum((w3 * w3).reshape(block // 8, 8, 128), axis=0)

    squares = lax.fori_loop(0, blocks, close, squares)

    part[...] = jnp.sum(squares, axis=0, keepdims=True)

    low = lax.rem(me, half)
    spot = high * nc + mycol

    def over_low(i, carry):
        to = low_peer(i)
        pltpu.make_async_remote_copy(
            part, secsum.at[low], r_ssem.at[2], r_rsem.at[2],
            device_id={"sector": high * half + to}, device_id_type=MESH,
        ).start()
        return carry

    lax.fori_loop(0, half - 1, over_low, 0, unroll=True)
    secsum[low] = part[...]
    most_low = pl.ds(0, half - 1)
    pltpu.make_async_remote_copy(
        secsum.at[most_low], secsum.at[most_low], r_ssem.at[2], r_rsem.at[2],
        device_id={"sector": nxt}, device_id_type=MESH,
    ).wait()
    secpart[...] = jnp.sum(secsum[...], axis=0)

    def over_high(i, carry):
        to_high, to = high_peer(i)
        pltpu.make_async_remote_copy(
            secpart, colsum.at[spot], a_ssem.at[2], a_rsem.at[2],
            device_id={"sector": low + half * to_high, "col": to},
            device_id_type=MESH,
        ).start()
        return carry

    lax.fori_loop(0, 2 * nc - 1, over_high, 0, unroll=True)
    colsum[spot] = secpart[...]
    most = pl.ds(0, 2 * nc - 1)
    pltpu.make_async_remote_copy(
        colsum.at[most], colsum.at[most], a_ssem.at[2], a_rsem.at[2],
        device_id={"sector": nxt}, device_id_type=MESH,
    ).wait()
    everything = jnp.sum(jnp.sum(colsum[...], axis=0), axis=1, keepdims=True)
    growth_ref[...] = jnp.broadcast_to(jnp.sqrt(everything / total_count + 1e-6), (1, 128))


def per_device(
    ns, nc, prev_nodes, stiffness, aero_coef, offset_slot, contact_left, contact_right, contact_mask
):
    cols = prev_nodes.shape[2]
    rows = cols * 8
    sectors = ns * LOCAL
    x = prev_nodes.reshape(8, cols, LOCAL, 2, 128).transpose(0, 1, 3, 2, 4).reshape(8, rows, 128)
    stiff = stiffness.reshape(LOCAL, 2, 128).transpose(1, 0, 2).reshape(8, 128)
    vm = pltpu.VMEM
    big = vm((rows, 128), F32)
    ints = vm((LOCAL, 128), jnp.int32)
    dma = pltpu.SemaphoreType.DMA
    any_spec = pl.BlockSpec(memory_space=pl.ANY)
    state, growth = pl.pallas_call(
        functools.partial(kernel, ns, nc, float(2 * cols * nc * sectors * DOF)),
        out_shape=(
            pltpu.VMEM((2, rows, 128), F32),
            pltpu.VMEM((1, 128), F32),
        ),
        in_specs=[any_spec] * 7,
        out_specs=(pl.BlockSpec(memory_space=pltpu.VMEM), pl.BlockSpec(memory_space=pltpu.VMEM)),
        scratch_shapes=[
            vm((8, rows, 128), F32),
            vm((8, 128), F32),
            vm((TABLES * AERO, AERO), BF16),
            vm((1, sectors), jnp.int32),
            ints, ints, ints,
            vm((8, 128), F32),
            vm((8, 128), F32),
            vm((LOCAL, 3 * DOF, DOF), BF16),
            vm((2, DOF, 128), BF16),
            vm((sectors, TABLES * sectors), BF16),
            vm((TABLES * sectors, 4 * AERO), BF16),
            big, big, big, big, big, big, big,
            big, big, big, big, big,
            vm((ns, 8, 256), BF16), vm((ns, 8, 256), BF16),
            vm((ns, 8, 128), BF16), vm((ns, 8, 128), BF16),
            vm((ns, 8, 256), BF16), vm((ns, 8, 256), BF16),
            vm((ns, 8, 128), BF16), vm((ns, 8, 128), BF16),
            vm((2, 3, cols + 16, 128), BF16), vm((2, 3, cols + 16, 128), BF16),
            vm((2, cols, 128), BF16), vm((2, cols, 128), BF16),
            vm((sectors, 2 * AERO), F32),
            vm((sectors, 4 * AERO), F32),
            vm((1, 128), F32),
            vm((2 * nc, 1, 128), F32),
            vm((ns // 2, 1, 128), F32),
            vm((1, 128), F32),
            dma((5,)), dma((5,)),
            dma((2, 3)), dma((2, 3)),
            dma((3,)), dma((3,)), dma((3,)), dma((3,)),
            dma((2,)), dma((2,)),
        ],
        compiler_params=pltpu.CompilerParams(
            collective_id=0, has_side_effects=True, vmem_limit_bytes=60 << 20
        ),
        name="sweep",
    )(
        x, stiff, aero_coef.reshape(TABLES * AERO, AERO), offset_slot.reshape(1, sectors),
        contact_left, contact_right, contact_mask,
    )
    value = growth[0, 0]
    scaled = state / value
    scaled = scaled.reshape(2, cols, 2, LOCAL, 128).transpose(0, 1, 3, 2, 4)
    return scaled.reshape(2, cols, LOCAL, DOF), value


def solution(mesh):
    ns, nc = mesh.shape["sector"], mesh.shape["col"]
    placed = (
        P(None, None, "col", "sector", None),
        P("sector", None),
        P(),
        P(),
        P("sector", None),
        P("sector", None),
        P("sector", None),
    )
    return jax.shard_map(
        functools.partial(per_device, ns, nc),
        mesh=mesh,
        in_specs=placed,
        out_specs=(P(None, "col", "sector", None), P()),
        check_vma=False,
    )
```
